128 devices in a mesh: member: 2 (over x_lo), dp: 64 (over y, x_hi, z, core).
Axes of the slice: x: 4 (x_hi: 2, x_lo: 2; x = x_hi * 2 + x_lo), y: 4, z: 4, core: 2. Of those that a mesh axis runs over, the one named last changes fastest.
Arguments:
- features: bfloat16 [256, 256, 1024], P(('dp', 'member')), may hold values from -10 to 10
- teacher_logits: bfloat16 [4, 256, 256, 256], P('member', 'dp'), may hold values from -320 to 320
- lengths: int32 [256], P(('dp', 'member')), may hold values from 16 to 256
- gain_conv: float32 [1024], replicated, may hold values from 0.5 to 1.5
- weight_in: bfloat16 [1024, 2048], replicated, may hold values from -0.1875 to 0.1875
- weight_depth: float32 [31, 1024], replicated, may hold values from -1 to 1
- weight_out: bfloat16 [1024, 1024], replicated, may hold values from -0.1875 to 0.1875
- gain_out: float32 [1024], replicated, may hold values from 0.5 to 1.5
- head_weight: bfloat16 [1024, 256], replicated, may hold values from -1 to 1
Outputs:
- grad_gain_conv: float32 [1024], replicated
- grad_weight_in: float32 [1024, 2048], replicated
- grad_weight_depth: float32 [31, 1024], replicated
- grad_weight_out: float32 [1024, 1024], replicated
- grad_gain_out: float32 [1024], replicated
- grad_head: float32 [1024, 256], replicated
- utt_loss: float32 [256], P(('dp', 'member'))
The draws below stay inside these ranges and needn't reach their ends.
All inputs are finite; a program needn't handle non-finite values.
Results may differ from the reference program's by a relative error of at most 0.015.
Values may be sent and summed in bfloat16 or wider, within the bound.
A program may use at most 128 MiB of HBM per device.

```python
import math
import jax
import jax.numpy as jnp
from jax import lax

D = 1024
V = 256
KERNEL = 31
TEACHERS = 4
LEN = 256
U_DEV = 2
UTTS = 256


def draw_features(key, part):
    values = jnp.clip(jax.random.normal(jax.random.fold_in(key, 1), (UTTS, LEN, D), jnp.float32), -6.0, 6.0)
    return values.astype(jnp.bfloat16)


def draw_head_weight(key, part):
    values = jax.random.normal(jax.random.fold_in(key, 2), (D, V), jnp.float32) * (1.0 / math.sqrt(D))
    return jnp.clip(values, -1.0, 1.0).astype(jnp.bfloat16)


def draw_teacher_logits(key, part):
    first_key = jax.random.fold_in(key, 0)
    base = 3.0 * jax.random.normal(first_key, (TEACHERS, UTTS, LEN, V), jnp.float32)
    return jnp.clip(base, -18.0, 18.0).astype(jnp.bfloat16)


def draw_lengths(key, part):
    utterance_index = jnp.arange(UTTS, dtype=jnp.int32)
    lowest = LEN // 16 + 3 * LEN // 4 * utterance_index // UTTS
    drawn = jax.random.randint(key, (UTTS,), 0, LEN // 4 + 1, dtype=jnp.int32) + lowest
    drawn = jnp.minimum(drawn, LEN)
    drawn = drawn.at[0].set(LEN // 16)
    return drawn.at[UTTS - 1].set(LEN)


def noise(own_key, extent, scale, limit, kind=jnp.bfloat16):
    return jnp.clip(scale * jax.random.normal(own_key, extent, jnp.float32), -limit, limit).astype(kind)


def setup_inputs(seed: int = 0) -> dict:
    splits = jax.random.split(jax.random.key(seed), 10)
    return {
        "features": draw_features(jax.random.fold_in(splits[9], 71), 0),
        "teacher_logits": draw_teacher_logits(jax.random.fold_in(splits[9], 71), 0),
        "lengths": draw_lengths(jax.random.fold_in(splits[9], 71), 0),
        "gain_conv": jnp.clip(1.0 + 0.1 * jax.random.normal(splits[3], (D,), jnp.float32), 0.5, 1.5),
        "weight_in": noise(splits[4], (D, 2 * D), D ** -0.5, 0.1875),
        "weight_depth": noise(splits[5], (KERNEL, D), KERNEL ** -0.5, 1.0, jnp.float32),
        "weight_out": noise(splits[6], (D, D), D ** -0.5, 0.1875),
        "gain_out": jnp.clip(1.0 + 0.1 * jax.random.normal(splits[7], (D,), jnp.float32), 0.5, 1.5),
        "head_weight": draw_head_weight(jax.random.fold_in(splits[9], 71), 0),
    }


def normalize(values, gain):
    average = lax.optimization_barrier(jnp.mean(values, axis=-1, keepdims=True))
    centred = values - average
    spread = lax.optimization_barrier(jnp.mean(centred * centred, axis=-1, keepdims=True))
    return centred * lax.rsqrt(spread + 1e-05) * gain

def live_frames(lengths, frames):
    return (jnp.arange(frames, dtype=jnp.int32)[None, :] < lengths[:, None]).astype(jnp.float32)

def depthwise(gated, weight_depth):
    frames = gated.shape[1]
    taps = weight_depth.shape[0]
    half_width = taps // 2
    padded = jnp.pad(gated, ((0, 0), (half_width, half_width), (0, 0)))
    total = jnp.zeros(gated.shape, gated.dtype)
    for offset in range(taps):
        total = total + weight_depth[offset][None, None, :] * padded[:, offset:offset + frames, :]
    return total

def lower_part(conv_weights, features, lengths):
    gain_conv, weight_in, weight_depth, weight_out = conv_weights
    utterances, frames, model_width = features.shape
    widened = features.astype(jnp.float32)
    normed = normalize(widened, gain_conv).astype(jnp.bfloat16).reshape(utterances * frames, model_width)
    projected = jnp.dot(normed, weight_in, preferred_element_type=jnp.float32)
    live_mask = live_frames(lengths, frames)
    gated = (projected[:, :model_width] * jax.nn.sigmoid(projected[:, model_width:])).reshape(utterances, frames, model_width) * live_mask[:, :, None]
    convolved = depthwise(gated, weight_depth)
    activated = (convolved * jax.nn.sigmoid(convolved)).astype(jnp.bfloat16).reshape(utterances * frames, model_width)
    update = jnp.dot(activated, weight_out, preferred_element_type=jnp.float32)
    return widened + update.reshape(utterances, frames, model_width)

def upper_part(top_weights, residual_sum, target, lengths, mean_frames):
    gain_out, head_weight = top_weights
    utterances, frames, model_width = residual_sum.shape
    final_norm = normalize(residual_sum, gain_out).astype(jnp.bfloat16).reshape(utterances * frames, model_width)
    student_logits = jnp.dot(final_norm, head_weight, preferred_element_type=jnp.float32)
    student_logp = jax.nn.log_softmax(student_logits, axis=-1).reshape(utterances, frames, -1)
    cross_entropy = -lax.optimization_barrier(jnp.sum(target * student_logp, axis=-1))
    return lax.optimization_barrier(jnp.sum(cross_entropy * live_frames(lengths, frames), axis=-1)) / mean_frames

def student_losses(weights, features, target, lengths, mean_frames):
    residual_sum = lower_part(weights[:4], features, lengths)
    return upper_part(weights[4:], residual_sum, target, lengths, mean_frames)

def teacher_target(summed):
    return jnp.exp(jax.nn.log_softmax(summed / TEACHERS, axis=-1))

def reference(features, teacher_logits, lengths, gain_conv, weight_in, weight_depth, weight_out, gain_out, head_weight):
    mean_frames = jnp.sum(lengths.astype(jnp.float32)) / UTTS
    weights = (gain_conv, weight_in, weight_depth, weight_out, gain_out, head_weight)

    def one_block(running, block_index):
        start = block_index * U_DEV
        block_features = lax.dynamic_slice_in_dim(features, start, U_DEV, 0)
        block_logits = lax.dynamic_slice_in_dim(teacher_logits, start, U_DEV, 1)
        block_lengths = lax.dynamic_slice_in_dim(lengths, start, U_DEV, 0)
        summed = lax.optimization_barrier(jnp.sum(jax.nn.log_softmax(block_logits.astype(jnp.float32), axis=-1), axis=0))
        target = teacher_target(summed)

        def local_loss(trainable):
            return student_losses(trainable, block_features, target, block_lengths, mean_frames)
        losses, pullback = jax.vjp(local_loss, weights)
        gradients = pullback(jnp.ones_like(losses))[0]
        updated = tuple((running_sum + piece_grad.astype(jnp.float32) for running_sum, piece_grad in zip(running, gradients)))
        return (updated, losses)
    initial = tuple((jnp.zeros(weight.shape, jnp.float32) for weight in weights))
    totals, losses = lax.scan(one_block, initial, jnp.arange(UTTS // U_DEV, dtype=jnp.int32))
    return (totals[0], totals[1], totals[2], totals[3], totals[4], totals[5], losses.reshape(UTTS))
```

```python
import functools
import math

import jax
import jax.numpy as jnp
import numpy as np
from jax import lax
from jax.experimental import pallas as pl
from jax.experimental.pallas import tpu as pltpu
from jax.sharding import PartitionSpec as P

D, V, TAPS, FRAMES, UTT = 1024, 256, 31, 256, 2
TOK = UTT * FRAMES
PERIOD, HALF, ROWS = 272, 144, 288
TILE = 256
SLABS = 28
F32, BF16 = jnp.float32, jnp.bfloat16
VM = pl.BlockSpec(memory_space=pltpu.VMEM)
SM = pl.BlockSpec(memory_space=pltpu.SMEM)


def transforms():
    freq = np.arange(PERIOD // 2 + 1)
    time = np.arange(FRAMES)
    angle = 2 * np.pi * np.outer(freq, time) / PERIOD
    analysis = np.zeros((ROWS, FRAMES))
    analysis[: freq.size] = np.cos(angle)
    analysis[HALF : HALF + freq.size] = np.sin(angle)
    lag = np.arange(TAPS) - TAPS // 2
    weight = np.where((freq == 0) | (freq == PERIOD // 2), 1.0, 2.0)[:, None] / PERIOD
    turn = 2 * np.pi * np.outer(freq, lag) / PERIOD
    taps = np.zeros((ROWS, TAPS + 1))
    taps[: freq.size, :TAPS] = np.cos(turn) * weight
    taps[HALF : HALF + freq.size, :TAPS] = np.sin(turn) * weight
    lags = np.zeros((ROWS, 128))
    lags[:, : TAPS + 1] = taps
    bf = lambda v: jnp.asarray(v, F32).astype(BF16)
    return bf(analysis), bf(analysis.T), jnp.asarray(taps, F32), bf(lags)


def dot(a, b):
    return jnp.dot(a, b, preferred_element_type=F32)


def dot_bt(a, b):
    return lax.dot_general(a, b, (((1,), (1,)), ((), ())), preferred_element_type=F32)


def dot_at(a, b):
    return lax.dot_general(a, b, (((0,), (0,)), ((), ())), preferred_element_type=F32)


def sigmoid(v):
    return 1.0 / (1.0 + jnp.exp(-v))


def rows_loop(total, step, body):
    def run(i, c):
        body(pl.ds(pl.multiple_of(i * step, step), step), i)
        return c

    lax.fori_loop(0, total // step, run, 0)


def forward_kernel(
    len_ref, x_ref, g1_ref, win_ref, taps_ref, wout_ref, g2_ref, head_ref, tm_ref, c_ref, ct_ref,
    normed_ref, a_ref, s_ref, spec_ref, fac_ref, act_ref, z_ref, rstd_ref, fn_ref, logit_ref,
    taps32, res,
):
    taps32[...] = jnp.zeros_like(taps32)
    taps32[0:TAPS, :] = taps_ref[...]

    def norm_rows(rows, i):
        v = x_ref[rows, :].astype(F32)
        v = v - jnp.mean(v, axis=-1, keepdims=True)
        v = v * lax.rsqrt(jnp.mean(v * v, axis=-1, keepdims=True) + 1e-5)
        normed_ref[rows, :] = (v * g1_ref[...]).astype(BF16)

    rows_loop(TOK, 32, norm_rows)

    def channel_tile(cb, carry):
        cols = pl.ds(pl.multiple_of(cb * TILE, TILE), TILE)
        gate_cols = pl.ds(pl.multiple_of(D + cb * TILE, TILE), TILE)
        hat = jnp.dot(
            tm_ref[...], taps32[:, cols], preferred_element_type=F32, precision=lax.Precision.HIGHEST
        )
        hr, hi = hat[:HALF], hat[HALF:]
        for u in range(UTT):
            rows = pl.ds(u * FRAMES, FRAMES)
            live = lax.broadcasted_iota(jnp.int32, (FRAMES, TILE), 0) < len_ref[u]
            nu = normed_ref[rows, :]
            a = dot(nu, win_ref[:, cols])
            s = sigmoid(dot(nu, win_ref[:, gate_cols]))
            a = jnp.where(live, a, 0.0)
            s_ref[rows, cols] = s.astype(BF16)
            a_ref[rows, cols] = a.astype(BF16)
            sp = dot(c_ref[...], (a * s).astype(BF16))
            spec_ref[u, :, cols] = sp.astype(BF16)
            xr, xi = sp[:HALF], sp[HALF:]
            prod = jnp.concatenate([xr * hr + xi * hi, xi * hr - xr * hi], axis=0)
            conv = dot(ct_ref[...], prod.astype(BF16))
            sg = sigmoid(conv)
            act_ref[rows, cols] = (conv * sg).astype(BF16)
            fac_ref[rows, cols] = (sg * (1.0 + conv * (1.0 - sg))).astype(BF16)
        return carry

    lax.fori_loop(0, D // TILE, channel_tile, 0)

    def out_tile(cb, carry):
        cols = pl.ds(pl.multiple_of(cb * TILE, TILE), TILE)
        res[:, cols] = x_ref[:, cols].astype(F32) + dot(act_ref[...], wout_ref[:, cols])
        return carry

    lax.fori_loop(0, D // TILE, out_tile, 0)

    def norm_out(rows, i):
        v = res[rows, :]
        v = v - jnp.mean(v, axis=-1, keepdims=True)
        r = lax.rsqrt(jnp.mean(v * v, axis=-1, keepdims=True) + 1e-5)
        z = v * r
        z_ref[rows, :] = z.astype(BF16)
        rstd_ref[rows, :] = jnp.broadcast_to(r, (32, 128))
        fn_ref[rows, :] = (z * g2_ref[...]).astype(BF16)

    rows_loop(TOK, 32, norm_out)
    logit_ref[...] = dot(fn_ref[...], head_ref[...])


def softmax_parts(v):
    m = jnp.max(v, axis=-1, keepdims=True)
    e = jnp.exp(v - m)
    return m, e, jnp.sum(e, axis=-1, keepdims=True)


def backward_kernel(
    len_ref, own_ref, got_ref, logit_ref, fn_ref, z_ref, rstd_ref, act_ref, fac_ref, spec_ref, s_ref, a_ref,
    normed_ref, win_ref, taps_ref, wout_ref, g2_ref, head_ref, tm_ref, c_ref, ct_ref, lag_ref,
    grad_ref, loss_ref,
    taps32, dl, dz, dr, dp, gain1, left,
):
    taps32[...] = jnp.zeros_like(taps32)
    taps32[0:TAPS, :] = taps_ref[...]
    gain1[...] = jnp.zeros_like(gain1)

    for u in range(UTT):
        length = len_ref[u]

        def loss_rows(i, total):
            rows = pl.ds(pl.multiple_of(i * 32, 32), 32)
            flat = pl.ds(pl.multiple_of(u * FRAMES + i * 32, 32), 32)
            summed = jnp.zeros((32, V), F32)
            for ref in (own_ref, got_ref):
                for k in range(2):
                    t = ref[k, u, rows, :].astype(F32)
                    m, _, z = softmax_parts(t)
                    summed = summed + (t - m - jnp.log(z))
            _, e, z = softmax_parts(summed * 0.25)
            target = e / z
            lg = logit_ref[flat, :]
            m, e, z = softmax_parts(lg)
            live = i * 32 + lax.broadcasted_iota(jnp.int32, (32, V), 0) < length
            ce = jnp.sum(jnp.where(live, target * (m + jnp.log(z) - lg), 0.0), axis=0, keepdims=True)
            mass = jnp.sum(target, axis=-1, keepdims=True)
            dl[flat, :] = jnp.where(live, e * (mass / z) - target, 0.0).astype(BF16)
            return total + ce

        total = lax.fori_loop(0, FRAMES // 32, loss_rows, jnp.zeros((1, V), F32))
        loss_ref[u : u + 1, :] = jnp.broadcast_to(jnp.sum(total, axis=-1, keepdims=True), (1, 128))

    def head_tile(cb, carry):
        cols = pl.ds(pl.multiple_of(cb * TILE, TILE), TILE)
        rows = cols
        dz[:, cols] = dot_bt(dl[...], head_ref[rows, :])
        dh = dot_at(fn_ref[:, cols], dl[...])
        grad_ref[24, rows, :] = dh[:, :128].astype(BF16)
        grad_ref[25, rows, :] = dh[:, 128:].astype(BF16)
        left[1, rows, :] = jnp.broadcast_to(
            jnp.sum(dh * head_ref[rows, :].astype(F32), axis=-1, keepdims=True), (TILE, 128)
        )
        return carry

    lax.fori_loop(0, D // TILE, head_tile, 0)

    def norm_rows(rows, i):
        g = dz[rows, :] * g2_ref[...]
        z = z_ref[rows, :].astype(F32)
        r = rstd_ref[rows, :][:, :1]
        m1 = jnp.mean(g, axis=-1, keepdims=True)
        m2 = jnp.mean(g * z, axis=-1, keepdims=True)
        dr[rows, :] = (r * (g - m1 - z * m2)).astype(BF16)

    rows_loop(TOK, 32, norm_rows)

    def conv_tile(cb, carry):
        cols = pl.ds(pl.multiple_of(cb * TILE, TILE), TILE)
        gate_cols = pl.ds(pl.multiple_of(D + cb * TILE, TILE), TILE)
        hat = jnp.dot(
            tm_ref[...], taps32[:, cols], preferred_element_type=F32, precision=lax.Precision.HIGHEST
        )
        hr, hi = hat[:HALF], hat[HALF:]
        q = jnp.zeros((ROWS, TILE), F32)
        for u in range(UTT):
            rows = pl.ds(u * FRAMES, FRAMES)
            dact = dot_bt(dr[rows, :], wout_ref[cols, :])
            dc = (dact * fac_ref[rows, cols].astype(F32)).astype(BF16)
            sp = dot(c_ref[...], dc)
            er, ei = sp[:HALF], sp[HALF:]
            x = spec_ref[u, :, cols].astype(F32)
            xr, xi = x[:HALF], x[HALF:]
            q = q + jnp.concatenate([er * xr + ei * xi, er * xi - ei * xr], axis=0)
            back = jnp.concatenate([er * hr - ei * hi, ei * hr + er * hi], axis=0)
            dg = dot(ct_ref[...], back.astype(BF16))
            live = lax.broadcasted_iota(jnp.int32, (FRAMES, TILE), 0) < len_ref[u]
            s = s_ref[rows, cols].astype(F32)
            a = a_ref[rows, cols].astype(F32)
            ds = jnp.where(live, dg * s, 0.0)
            dp[rows, cols] = ds.astype(BF16)
            dp[rows, gate_cols] = (ds * a * (1.0 - s)).astype(BF16)
        left[0, cols, :] = dot_at(q.astype(BF16), lag_ref[...])
        dw = dot_at(act_ref[:, cols], dr[...])
        for j in range(8):
            grad_ref[16 + j, cols, :] = dw[:, j * 128 : (j + 1) * 128].astype(BF16)
        return carry

    lax.fori_loop(0, D // TILE, conv_tile, 0)

    def in_tile(n, carry):
        cols = pl.ds(pl.multiple_of(n * TILE, TILE), TILE)
        dw = dot_at(normed_ref[...], dp[:, cols])
        grad_ref[2 * n] = dw[:, :128].astype(BF16)
        grad_ref[2 * n + 1] = dw[:, 128:].astype(BF16)
        w = dw * win_ref[:, cols].astype(F32)
        gain1[...] += w[:, :128] + w[:, 128:]
        return carry

    lax.fori_loop(0, 2 * D // TILE, in_tile, 0)

    count = len_ref[0] + len_ref[1]

    def small_rows(rows, i):
        lane = lax.broadcasted_iota(jnp.int32, (128, 128), 1)
        bit = jnp.right_shift(count, jnp.clip(lane - 64, 0, 15)) & 1
        g1 = jnp.sum(gain1[rows, :], axis=-1, keepdims=True)
        out = jnp.where(lane < TAPS, left[0, rows, :], 0.0)
        out = jnp.where(lane == 32, g1, out)
        out = jnp.where(lane == 33, left[1, rows, :], out)
        out = jnp.where((lane >= 64) & (lane < 74), bit.astype(F32), out)
        grad_ref[26, rows, :] = out.astype(BF16)
        grad_ref[27, rows, :] = jnp.zeros((128, 128), BF16)

    rows_loop(D, 128, small_rows)


def compute(features, own, got, lengths, gain_conv, weight_in, weight_depth, weight_out, gain_out, head):
    analysis, synthesis, tapm, lagm = transforms()
    sd = jax.ShapeDtypeStruct
    cp = pltpu.CompilerParams(vmem_limit_bytes=60 << 20)
    g1, g2 = gain_conv.reshape(1, D), gain_out.reshape(1, D)
    fwd = pl.pallas_call(
        forward_kernel,
        name="forward",
        out_shape=(
            sd((TOK, D), BF16), sd((TOK, D), BF16), sd((TOK, D), BF16), sd((UTT, ROWS, D), BF16),
            sd((TOK, D), BF16), sd((TOK, D), BF16), sd((TOK, D), BF16), sd((TOK, 128), F32),
            sd((TOK, D), BF16), sd((TOK, V), F32),
        ),
        in_specs=[SM] + [VM] * 10,
        out_specs=[VM] * 10,
        scratch_shapes=[pltpu.VMEM((32, D), F32), pltpu.VMEM((TOK, D), F32)],
        compiler_params=cp,
        cost_estimate=pl.CostEstimate(flops=4 * 10**9, bytes_accessed=20 << 20, transcendentals=2 << 20),
    )
    normed, a, s, spec, fac, act, z, rstd, fn, logit = fwd(
        lengths, features.reshape(TOK, D), g1, weight_in, weight_depth, weight_out, g2, head,
        tapm, analysis, synthesis,
    )
    bwd = pl.pallas_call(
        backward_kernel,
        name="backward",
        out_shape=(sd((SLABS, D, 128), BF16), sd((UTT, 128), F32)),
        in_specs=[SM] + [VM] * 21,
        out_specs=[VM] * 2,
        scratch_shapes=[
            pltpu.VMEM((32, D), F32), pltpu.VMEM((TOK, V), BF16), pltpu.VMEM((TOK, D), F32),
            pltpu.VMEM((TOK, D), BF16), pltpu.VMEM((TOK, 2 * D), BF16), pltpu.VMEM((D, 128), F32),
            pltpu.VMEM((2, D, 128), F32),
        ],
        compiler_params=cp,
    )
    return bwd(
        lengths, own, got, logit, fn, z, rstd, act, fac, spec, s, a, normed, weight_in, weight_depth,
        weight_out, g2, head, tapm, analysis, synthesis, lagm,
    )


MESH = pl.DeviceIdType.MESH
COUNTS = (3, 3, 2, 2, 2, 2)
OFFSETS = (0, 3, 6, 8, 10, 12)
OWN = 14
ROUNDS = 6


def position():
    member, dp = lax.axis_index("member"), lax.axis_index("dp")
    core, z, rest = dp % 2, (dp // 2) % 4, dp // 8
    return ((rest % 2) * 2 + member, rest // 2, z), core


def device(coords, core):
    x, y, z = coords
    return {"member": x % 2, "dp": ((y * 2 + x // 2) * 4 + z) * 2 + core}


def other(c, wide):
    return 3 - c if wide else c + 1 - 2 * (c % 2)


def kept(c, kind, second):
    if kind == 0 and not second:
        return (c + c // 2) % 2
    return c % 2 if (kind == 1 and second) else c // 2


def route(coords, core, s, k):
    dim = (s // 2 + core + k // 2) % 3
    hit = [jnp.where(dim == d, 1, 0) for d in range(3)]
    c = sum(h * v for h, v in zip(hit, coords))
    kind, second = s % 2, k % 2
    p = other(c, (kind + second) % 2 == 1)
    peer = [v + h * (p - v) for h, v in zip(hit, coords)]
    return device(peer, core), kept(c, kind, second == 1)


def reduce_kernel(
    grad_ref, out_ref, pair_buf, work, *rest
):
    bufs = rest[:ROUNDS]
    pair_s, pair_r, rs_s, rs_r, ag_s, ag_r, fin_s, fin_r = rest[ROUNDS:]
    coords, core = position()
    partner = device(coords, 1 - core)
    mine = core * OWN
    theirs = (1 - core) * OWN

    barrier = pltpu.get_barrier_semaphore()
    greet = [partner]
    for d in range(3):
        for wide in (False, True):
            greet.append(device([other(v, wide) if i == d else v for i, v in enumerate(coords)], core))
    for dev in greet:
        pl.semaphore_signal(barrier, inc=1, device_id=dev, device_id_type=MESH)
    pl.semaphore_wait(barrier, len(greet))

    def copy(src, dst, send, recv, dev):
        return pltpu.make_async_remote_copy(
            src_ref=src, dst_ref=dst, send_sem=send, recv_sem=recv, device_id=dev, device_id_type=MESH
        )

    pending = []
    pairs = []
    for s in range(6):
        off, n = OFFSETS[s], COUNTS[s]
        c = copy(
            grad_ref.at[pl.ds(theirs + off, n)], pair_buf.at[pl.ds(off, n)], pair_s.at[s], pair_r.at[s], partner
        )
        c.start()
        pairs.append(c)

    starts = [jnp.int32(0)] * 6
    history = [[] for _ in range(6)]
    flying = [None] * 6

    def launch(s, k):
        half = 512 >> k
        dev, keep = route(coords, core, s, k)
        slots = pl.ds(OFFSETS[s], COUNTS[s])
        give = pl.multiple_of(starts[s] + (1 - keep) * half, 16)
        c = copy(
            work.at[slots, pl.ds(give, half)],
            bufs[k].at[pl.ds(OFFSETS[s], COUNTS[s])],
            rs_s.at[s, k], rs_r.at[s, k], dev,
        )
        c.start()
        flying[s] = c
        pending.append(c)
        starts[s] = starts[s] + keep * half
        history[s].append(dev)

    def add(dst_ref, dst_slot, dst_row, a_ref, a_slot, a_row, b_ref, b_slot, n, size):
        step = min(size, 128)

        def run(i, carry):
            r = i * step
            for j in range(n):
                d = pl.ds(pl.multiple_of(dst_row + r, 16), step)
                a = a_ref[a_slot + j, pl.ds(pl.multiple_of(a_row + r, 16), step), :]
                b = b_ref[b_slot + j, pl.ds(pl.multiple_of(r, 16), step), :]
                dst_ref[dst_slot + j, d, :] = a + b
            return carry

        lax.fori_loop(0, size // step, run, 0)

    for s in range(6):
        off, n = OFFSETS[s], COUNTS[s]
        pairs[s].wait_recv()
        add(work, off, 0, grad_ref, mine + off, 0, pair_buf, off, n, D)
        launch(s, 0)

    for k in range(ROUNDS):
        half = 512 >> k
        for s in range(6):
            off, n = OFFSETS[s], COUNTS[s]
            flying[s].wait_recv()
            if k + 1 < ROUNDS:
                add(work, off, starts[s], work, off, starts[s], bufs[k], off, n, half)
                launch(s, k + 1)
            else:
                add(out_ref, mine + off, starts[s], work, off, starts[s], bufs[k], off, n, half)
                gather(s, k, copy, out_ref, mine, starts, history, ag_s, ag_r, flying, pending)

    for k in range(ROUNDS - 1, -1, -1):
        half = 512 >> k
        for s in range(6):
            flying[s].wait_recv()
            _, keep = route(coords, core, s, k)
            starts[s] = starts[s] - keep * half
            if k > 0:
                gather(s, k - 1, copy, out_ref, mine, starts, history, ag_s, ag_r, flying, pending)
            else:
                slots = pl.ds(mine + OFFSETS[s], COUNTS[s])
                c = copy(out_ref.at[slots], out_ref.at[slots], fin_s.at[s], fin_r.at[s], partner)
                c.start()
                pending.append(c)
                flying[s] = c
    for s in range(6):
        flying[s].wait_recv()
        pairs[s].wait_send()
    for c in pending:
        c.wait_send()


def gather(s, k, copy, out_ref, mine, starts, history, ag_s, ag_r, flying, pending):
    half = 512 >> k
    slots = pl.ds(mine + OFFSETS[s], COUNTS[s])
    span = pl.ds(pl.multiple_of(starts[s], 16), half)
    c = copy(
        out_ref.at[slots, span], out_ref.at[slots, span], ag_s.at[s, k], ag_r.at[s, k], history[s][k]
    )
    c.start()
    flying[s] = c
    pending.append(c)


def reduce_all(grads):
    dma = pltpu.SemaphoreType.DMA
    return pl.pallas_call(
        reduce_kernel,
        name="reduce_all",
        out_shape=jax.ShapeDtypeStruct((SLABS, D, 128), BF16),
        in_specs=[VM],
        out_specs=VM,
        scratch_shapes=[pltpu.VMEM((OWN, D, 128), BF16)] * 2
        + [pltpu.VMEM((OWN, 512 >> k, 128), BF16) for k in range(ROUNDS)]
        + [dma((6,)), dma((6,))] + [dma((6, ROUNDS))] * 4 + [dma((6,)), dma((6,))],
        compiler_params=pltpu.CompilerParams(
            collective_id=0, has_side_effects=True, vmem_limit_bytes=48 << 20
        ),
    )(grads)


def finish_kernel(
    in_ref, mid_ref, head_ref, small_ref, loss_ref, g1_ref, g2_ref,
    win_ref, wout_ref, hw_ref, depth_ref, gain1_ref, gain2_ref, utt_ref, scale,
):
    @pl.when(pl.program_id(0) == 0)
    def _():
        first = small_ref[0, 0:16, :].astype(F32)[0:1, :]
        lane = lax.broadcasted_iota(jnp.int32, (1, 128), 1)
        place = jnp.left_shift(1, jnp.clip(lane - 64, 0, 12)).astype(F32)
        used = (lane >= 64) & (lane < 74)
        count = jnp.sum(jnp.where(used, first * place, 0.0), axis=-1, keepdims=True)
        inv = UTTS / count
        scale[...] = jnp.broadcast_to(inv, (8, 128))
        utt_ref[...] = loss_ref[...] * inv
        small = small_ref[0].astype(F32).T * inv
        depth_ref[...] = small[0:TAPS, :]
        gain1_ref[...] = small[32:33, :] / g1_ref[...]
        gain2_ref[...] = small[33:34, :] / g2_ref[...]

    inv = scale[0:1, :]
    for j in range(2):
        win_ref[:, j * 128 : (j + 1) * 128] = in_ref[j].astype(F32) * inv
        hw_ref[:, j * 128 : (j + 1) * 128] = head_ref[j].astype(F32) * inv
    wout_ref[...] = mid_ref[0].astype(F32) * inv


UTTS = 256.0


def finish(total, loss, gain_conv, gain_out):
    sd = jax.ShapeDtypeStruct
    whole = lambda *shape: pl.BlockSpec(shape, lambda i: (0,) * len(shape))
    outs = pl.pallas_call(
        finish_kernel,
        name="finish",
        grid=(8,),
        out_shape=(
            sd((D, 2 * D), F32), sd((D, D), F32), sd((D, V), F32), sd((TAPS, D), F32),
            sd((1, D), F32), sd((1, D), F32), sd((UTT, 128), F32),
        ),
        in_specs=[
            pl.BlockSpec((2, D, 128), lambda i: (i, 0, 0)),
            pl.BlockSpec((1, D, 128), lambda i: (16 + i, 0, 0)),
            pl.BlockSpec((2, 128, 128), lambda i: (12, i, 0)),
            pl.BlockSpec((1, D, 128), lambda i: (26, 0, 0)),
            whole(UTT, 128), whole(1, D), whole(1, D),
        ],
        out_specs=[
            pl.BlockSpec((D, 256), lambda i: (0, i)),
            pl.BlockSpec((D, 128), lambda i: (0, i)),
            pl.BlockSpec((128, V), lambda i: (i, 0)),
            whole(TAPS, D), whole(1, D), whole(1, D), whole(UTT, 128),
        ],
        scratch_shapes=[pltpu.VMEM((8, 128), F32)],
    )(total, total, total, total, loss, gain_conv.reshape(1, D), gain_out.reshape(1, D))
    win, wout, hw, depth, gain1, gain2, utt = outs
    return gain1.reshape(D), win, depth, wout, gain2.reshape(D), hw, utt[:, 0]


def on_device(
    features, teacher_logits, lengths, gain_conv, weight_in, weight_depth, weight_out, gain_out, head_weight
):
    member = lax.axis_index("member")
    give = lax.dynamic_slice_in_dim(teacher_logits, (1 - member) * UTT, UTT, 1)
    own = lax.dynamic_slice_in_dim(teacher_logits, member * UTT, UTT, 1)
    got = lax.ppermute(give, "member", ((0, 1), (1, 0)))
    grads, loss = compute(
        features, own, got, lengths, gain_conv, weight_in, weight_depth, weight_out, gain_out, head_weight
    )
    return finish(reduce_all(grads), loss, gain_conv, gain_out)


def solution(mesh):
    in_specs = (
        P(("dp", "member"), None, None), P("member", "dp", None, None), P(("dp", "member")),
        P(), P(), P(), P(), P(), P(),
    )
    out_specs = (P(), P(), P(), P(), P(), P(), P(("dp", "member")))
    return jax.shard_map(on_device, mesh=mesh, in_specs=in_specs, out_specs=out_specs, check_vma=False)
```

```python
import functools
import math

import jax
import jax.numpy as jnp
import numpy as np
from jax import lax
from jax.experimental import pallas as pl
from jax.experimental.pallas import tpu as pltpu
from jax.sharding import PartitionSpec as P

D, V, TAPS, FRAMES, UTT = 1024, 256, 31, 256, 2
TOK = UTT * FRAMES
PERIOD, HALF, ROWS = 272, 144, 288
TILE = 256
SLABS = 28
F32, BF16 = jnp.float32, jnp.bfloat16
VM = pl.BlockSpec(memory_space=pltpu.VMEM)
SM = pl.BlockSpec(memory_space=pltpu.SMEM)


def transforms():
    freq = np.arange(PERIOD // 2 + 1)
    time = np.arange(FRAMES)
    angle = 2 * np.pi * np.outer(freq, time) / PERIOD
    analysis = np.zeros((ROWS, FRAMES))
    analysis[: freq.size] = np.cos(angle)
    analysis[HALF : HALF + freq.size] = np.sin(angle)
    lag = np.arange(TAPS) - TAPS // 2
    weight = np.where((freq == 0) | (freq == PERIOD // 2), 1.0, 2.0)[:, None] / PERIOD
    turn = 2 * np.pi * np.outer(freq, lag) / PERIOD
    taps = np.zeros((ROWS, TAPS + 1))
    taps[: freq.size, :TAPS] = np.cos(turn) * weight
    taps[HALF : HALF + freq.size, :TAPS] = np.sin(turn) * weight
    lags = np.zeros((ROWS, 128))
    lags[:, : TAPS + 1] = taps
    bf = lambda v: jnp.asarray(v, F32).astype(BF16)
    return bf(analysis), bf(analysis.T), jnp.asarray(taps, F32), bf(lags)


def dot(a, b):
    return jnp.dot(a, b, preferred_element_type=F32)


def dot_bt(a, b):
    return lax.dot_general(a, b, (((1,), (1,)), ((), ())), preferred_element_type=F32)


def dot_at(a, b):
    return lax.dot_general(a, b, (((0,), (0,)), ((), ())), preferred_element_type=F32)


def sigmoid(v):
    return 1.0 / (1.0 + jnp.exp(-v))


def rows_loop(total, step, body):
    def run(i, c):
        body(pl.ds(pl.multiple_of(i * step, step), step), i)
        return c

    lax.fori_loop(0, total // step, run, 0)


def forward_kernel(
    len_ref, x_ref, g1_ref, win_ref, taps_ref, wout_ref, g2_ref, head_ref, tm_ref, c_ref, ct_ref,
    normed_ref, a_ref, s_ref, spec_ref, fac_ref, act_ref, z_ref, rstd_ref, fn_ref, logit_ref,
    taps32, res,
):
    taps32[...] = jnp.zeros_like(taps32)
    taps32[0:TAPS, :] = taps_ref[...]

    def norm_rows(rows, i):
        v = x_ref[rows, :].astype(F32)
        v = v - jnp.mean(v, axis=-1, keepdims=True)
        v = v * lax.rsqrt(jnp.mean(v * v, axis=-1, keepdims=True) + 1e-5)
        normed_ref[rows, :] = (v * g1_ref[...]).astype(BF16)

    rows_loop(TOK, 32, norm_rows)

    def channel_tile(cb, carry):
        cols = pl.ds(pl.multiple_of(cb * TILE, TILE), TILE)
        gate_cols = pl.ds(pl.multiple_of(D + cb * TILE, TILE), TILE)
        hat = jnp.dot(
            tm_ref[...], taps32[:, cols], preferred_element_type=F32, precision=lax.Precision.HIGHEST
        )
        hr, hi = hat[:HALF], hat[HALF:]
        for u in range(UTT):
            rows = pl.ds(u * FRAMES, FRAMES)
            live = lax.broadcasted_iota(jnp.int32, (FRAMES, TILE), 0) < len_ref[u]
            nu = normed_ref[rows, :]
            a = dot(nu, win_ref[:, cols])
            s = sigmoid(dot(nu, win_ref[:, gate_cols]))
            a = jnp.where(live, a, 0.0)
            s_ref[rows, cols] = s.astype(BF16)
            a_ref[rows, cols] = a.astype(BF16)
            sp = dot(c_ref[...], (a * s).astype(BF16))
            spec_ref[u, :, cols] = sp.astype(BF16)
            xr, xi = sp[:HALF], sp[HALF:]
            prod = jnp.concatenate([xr * hr + xi * hi, xi * hr - xr * hi], axis=0)
            conv = dot(ct_ref[...], prod.astype(BF16))
            sg = sigmoid(conv)
            act_ref[rows, cols] = (conv * sg).astype(BF16)
            fac_ref[rows, cols] = (sg * (1.0 + conv * (1.0 - sg))).astype(BF16)
        return carry

    lax.fori_loop(0, D // TILE, channel_tile, 0)

    def out_tile(cb, carry):
        cols = pl.ds(pl.multiple_of(cb * TILE, TILE), TILE)
        res[:, cols] = x_ref[:, cols].astype(F32) + dot(act_ref[...], wout_ref[:, cols])
        return carry

    lax.fori_loop(0, D // TILE, out_tile, 0)

    def norm_out(rows, i):
        v = res[rows, :]
        v = v - jnp.mean(v, axis=-1, keepdims=True)
        r = lax.rsqrt(jnp.mean(v * v, axis=-1, keepdims=True) + 1e-5)
        z = v * r
        z_ref[rows, :] = z.astype(BF16)
        rstd_ref[rows, :] = jnp.broadcast_to(r, (32, 128))
        fn_ref[rows, :] = (z * g2_ref[...]).astype(BF16)

    rows_loop(TOK, 32, norm_out)
    logit_ref[...] = dot(fn_ref[...], head_ref[...])


def softmax_parts(v):
    m = jnp.max(v, axis=-1, keepdims=True)
    e = jnp.exp(v - m)
    return m, e, jnp.sum(e, axis=-1, keepdims=True)


def backward_kernel(
    len_ref, own_ref, got_ref, logit_ref, fn_ref, z_ref, rstd_ref, act_ref, fac_ref, spec_ref, s_ref, a_ref,
    normed_ref, win_ref, taps_ref, wout_ref, g2_ref, head_ref, tm_ref, c_ref, ct_ref, lag_ref,
    grad_ref, loss_ref,
    taps32, dl, dz, dr, dp, gain1, left,
):
    taps32[...] = jnp.zeros_like(taps32)
    taps32[0:TAPS, :] = taps_ref[...]
    gain1[...] = jnp.zeros_like(gain1)

    for u in range(UTT):
        length = len_ref[u]

        def loss_rows(i, total):
            rows = pl.ds(pl.multiple_of(i * 32, 32), 32)
            flat = pl.ds(pl.multiple_of(u * FRAMES + i * 32, 32), 32)
            summed = jnp.zeros((32, V), F32)
            for ref in (own_ref, got_ref):
                for k in range(2):
                    t = ref[k, u, rows, :].astype(F32)
                    m, _, z = softmax_parts(t)
                    summed = summed + (t - m - jnp.log(z))
            _, e, z = softmax_parts(summed * 0.25)
            target = e / z
            lg = logit_ref[flat, :]
            m, e, z = softmax_parts(lg)
            live = i * 32 + lax.broadcasted_iota(jnp.int32, (32, V), 0) < length
            ce = jnp.sum(jnp.where(live, target * (m + jnp.log(z) - lg), 0.0), axis=0, keepdims=True)
            mass = jnp.sum(target, axis=-1, keepdims=True)
            dl[flat, :] = jnp.where(live, e * (mass / z) - target, 0.0).astype(BF16)
            return total + ce

        total = lax.fori_loop(0, FRAMES // 32, loss_rows, jnp.zeros((1, V), F32))
        loss_ref[u : u + 1, :] = jnp.broadcast_to(jnp.sum(total, axis=-1, keepdims=True), (1, 128))

    def head_tile(cb, carry):
        cols = pl.ds(pl.multiple_of(cb * TILE, TILE), TILE)
        rows = cols
        dz[:, cols] = dot_bt(dl[...], head_ref[rows, :])
        dh = dot_at(fn_ref[:, cols], dl[...])
        grad_ref[24, rows, :] = dh[:, :128].astype(BF16)
        grad_ref[25, rows, :] = dh[:, 128:].astype(BF16)
        left[1, rows, :] = jnp.broadcast_to(
            jnp.sum(dh * head_ref[rows, :].astype(F32), axis=-1, keepdims=True), (TILE, 128)
        )
        return carry

    lax.fori_loop(0, D // TILE, head_tile, 0)

    def norm_rows(rows, i):
        g = dz[rows, :] * g2_ref[...]
        z = z_ref[rows, :].astype(F32)
        r = rstd_ref[rows, :][:, :1]
        m1 = jnp.mean(g, axis=-1, keepdims=True)
        m2 = jnp.mean(g * z, axis=-1, keepdims=True)
        dr[rows, :] = (r * (g - m1 - z * m2)).astype(BF16)

    rows_loop(TOK, 32, norm_rows)

    def conv_tile(cb, carry):
        cols = pl.ds(pl.multiple_of(cb * TILE, TILE), TILE)
        gate_cols = pl.ds(pl.multiple_of(D + cb * TILE, TILE), TILE)
        hat = jnp.dot(
            tm_ref[...], taps32[:, cols], preferred_element_type=F32, precision=lax.Precision.HIGHEST
        )
        hr, hi = hat[:HALF], hat[HALF:]
        q = jnp.zeros((ROWS, TILE), F32)
        for u in range(UTT):
            rows = pl.ds(u * FRAMES, FRAMES)
            dact = dot_bt(dr[rows, :], wout_ref[cols, :])
            dc = (dact * fac_ref[rows, cols].astype(F32)).astype(BF16)
            sp = dot(c_ref[...], dc)
            er, ei = sp[:HALF], sp[HALF:]
            x = spec_ref[u, :, cols].astype(F32)
            xr, xi = x[:HALF], x[HALF:]
            q = q + jnp.concatenate([er * xr + ei * xi, er * xi - ei * xr], axis=0)
            back = jnp.concatenate([er * hr - ei * hi, ei * hr + er * hi], axis=0)
            dg = dot(ct_ref[...], back.astype(BF16))
            live = lax.broadcasted_iota(jnp.int32, (FRAMES, TILE), 0) < len_ref[u]
            s = s_ref[rows, cols].astype(F32)
            a = a_ref[rows, cols].astype(F32)
            ds = jnp.where(live, dg * s, 0.0)
            dp[rows, cols] = ds.astype(BF16)
            dp[rows, gate_cols] = (ds * a * (1.0 - s)).astype(BF16)
        left[0, cols, :] = dot_at(q.astype(BF16), lag_ref[...])
        dw = dot_at(act_ref[:, cols], dr[...])
        for j in range(8):
            grad_ref[16 + j, cols, :] = dw[:, j * 128 : (j + 1) * 128].astype(BF16)
        return carry

    lax.fori_loop(0, D // TILE, conv_tile, 0)

    def in_tile(n, carry):
        cols = pl.ds(pl.multiple_of(n * TILE, TILE), TILE)
        dw = dot_at(normed_ref[...], dp[:, cols])
        grad_ref[2 * n] = dw[:, :128].astype(BF16)
        grad_ref[2 * n + 1] = dw[:, 128:].astype(BF16)
        w = dw * win_ref[:, cols].astype(F32)
        gain1[...] += w[:, :128] + w[:, 128:]
        return carry

    lax.fori_loop(0, 2 * D // TILE, in_tile, 0)

    count = len_ref[0] + len_ref[1]

    def small_rows(rows, i):
        lane = lax.broadcasted_iota(jnp.int32, (128, 128), 1)
        bit = jnp.right_shift(count, jnp.clip(lane - 64, 0, 15)) & 1
        g1 = jnp.sum(gain1[rows, :], axis=-1, keepdims=True)
        out = jnp.where(lane < TAPS, left[0, rows, :], 0.0)
        out = jnp.where(lane == 32, g1, out)
        out = jnp.where(lane == 33, left[1, rows, :], out)
        out = jnp.where((lane >= 64) & (lane < 74), bit.astype(F32), out)
        grad_ref[26, rows, :] = out.astype(BF16)
        grad_ref[27, rows, :] = jnp.zeros((128, 128), BF16)

    rows_loop(D, 128, small_rows)


def compute(features, own, got, lengths, gain_conv, weight_in, weight_depth, weight_out, gain_out, head):
    analysis, synthesis, tapm, lagm = transforms()
    sd = jax.ShapeDtypeStruct
    cp = pltpu.CompilerParams(vmem_limit_bytes=60 << 20)
    g1, g2 = gain_conv.reshape(1, D), gain_out.reshape(1, D)
    fwd = pl.pallas_call(
        forward_kernel,
        name="forward",
        out_shape=(
            sd((TOK, D), BF16), sd((TOK, D), BF16), sd((TOK, D), BF16), sd((UTT, ROWS, D), BF16),
            sd((TOK, D), BF16), sd((TOK, D), BF16), sd((TOK, D), BF16), sd((TOK, 128), F32),
            sd((TOK, D), BF16), sd((TOK, V), F32),
        ),
        in_specs=[SM] + [VM] * 10,
        out_specs=[VM] * 10,
        scratch_shapes=[pltpu.VMEM((32, D), F32), pltpu.VMEM((TOK, D), F32)],
        compiler_params=cp,
        cost_estimate=pl.CostEstimate(flops=4 * 10**9, bytes_accessed=20 << 20, transcendentals=2 << 20),
    )
    normed, a, s, spec, fac, act, z, rstd, fn, logit = fwd(
        lengths, features.reshape(TOK, D), g1, weight_in, weight_depth, weight_out, g2, head,
        tapm, analysis, synthesis,
    )
    bwd = pl.pallas_call(
        backward_kernel,
        name="backward",
        out_shape=(sd((SLABS, D, 128), BF16), sd((UTT, 128), F32)),
        in_specs=[SM] + [VM] * 21,
        out_specs=[VM] * 2,
        scratch_shapes=[
            pltpu.VMEM((32, D), F32), pltpu.VMEM((TOK, V), BF16), pltpu.VMEM((TOK, D), F32),
            pltpu.VMEM((TOK, D), BF16), pltpu.VMEM((TOK, 2 * D), BF16), pltpu.VMEM((D, 128), F32),
            pltpu.VMEM((2, D, 128), F32),
        ],
        compiler_params=cp,
    )
    return bwd(
        lengths, own, got, logit, fn, z, rstd, act, fac, spec, s, a, normed, weight_in, weight_depth,
        weight_out, g2, head, tapm, analysis, synthesis, lagm,
    )


MESH = pl.DeviceIdType.MESH
STREAMS = 12
COUNTS = (2, 1, 1, 1, 1, 1, 1, 2, 1, 1, 1, 1)
OFFSETS = (0, 2, 3, 4, 5, 6, 7, 8, 10, 11, 12, 13)
OWN = 14
ROUNDS = 6


def position():
    member, dp = lax.axis_index("member"), lax.axis_index("dp")
    core, z, rest = dp % 2, (dp // 2) % 4, dp // 8
    return ((rest % 2) * 2 + member, rest // 2, z), core


def device(coords, core):
    x, y, z = coords
    return {"member": x % 2, "dp": ((y * 2 + x // 2) * 4 + z) * 2 + core}


def other(c, wide):
    return 3 - c if wide else c + 1 - 2 * (c % 2)


def kept(c, kind, second):
    if kind == 0 and not second:
        return (c + c // 2) % 2
    return c % 2 if (kind == 1 and second) else c // 2


def route(coords, core, s, k):
    s = s % 6
    dim = (s // 2 + core + k // 2) % 3
    hit = [jnp.where(dim == d, 1, 0) for d in range(3)]
    c = sum(h * v for h, v in zip(hit, coords))
    kind, second = s % 2, k % 2
    p = other(c, (kind + second) % 2 == 1)
    peer = [v + h * (p - v) for h, v in zip(hit, coords)]
    return device(peer, core), kept(c, kind, second == 1)


def reduce_kernel(
    grad_ref, out_ref, pair_buf, work, *rest
):
    bufs = rest[:ROUNDS]
    pair_s, pair_r, rs_s, rs_r, ag_s, ag_r, fin_s, fin_r = rest[ROUNDS:]
    coords, core = position()
    partner = device(coords, 1 - core)
    mine = core * OWN
    theirs = (1 - core) * OWN

    barrier = pltpu.get_barrier_semaphore()
    greet = [partner]
    for d in range(3):
        for wide in (False, True):
            greet.append(device([other(v, wide) if i == d else v for i, v in enumerate(coords)], core))
    for dev in greet:
        pl.semaphore_signal(barrier, inc=1, device_id=dev, device_id_type=MESH)
    pl.semaphore_wait(barrier, len(greet))

    def copy(src, dst, send, recv, dev):
        return pltpu.make_async_remote_copy(
            src_ref=src, dst_ref=dst, send_sem=send, recv_sem=recv, device_id=dev, device_id_type=MESH
        )

    pending = []
    pairs = []
    for s in range(STREAMS):
        off, n = OFFSETS[s], COUNTS[s]
        c = copy(
            grad_ref.at[pl.ds(theirs + off, n)], pair_buf.at[pl.ds(off, n)], pair_s.at[s], pair_r.at[s], partner
        )
        c.start()
        pairs.append(c)

    starts = [jnp.int32(0)] * STREAMS
    history = [[] for _ in range(STREAMS)]
    flying = [None] * STREAMS

    def launch(s, k):
        half = 512 >> k
        dev, keep = route(coords, core, s, k)
        slots = pl.ds(OFFSETS[s], COUNTS[s])
        give = pl.multiple_of(starts[s] + (1 - keep) * half, 16)
        c = copy(
            work.at[slots, pl.ds(give, half)],
            bufs[k].at[pl.ds(OFFSETS[s], COUNTS[s])],
            rs_s.at[s, k], rs_r.at[s, k], dev,
        )
        c.start()
        flying[s] = c
        pending.append(c)
        starts[s] = starts[s] + keep * half
        history[s].append(dev)

    def add(dst_ref, dst_slot, dst_row, a_ref, a_slot, a_row, b_ref, b_slot, n, size):
        step = min(size, 128)

        def run(i, carry):
            r = i * step
            for j in range(n):
                d = pl.ds(pl.multiple_of(dst_row + r, 16), step)
                a = a_ref[a_slot + j, pl.ds(pl.multiple_of(a_row + r, 16), step), :]
                b = b_ref[b_slot + j, pl.ds(pl.multiple_of(r, 16), step), :]
                dst_ref[dst_slot + j, d, :] = a + b
            return carry

        lax.fori_loop(0, size // step, run, 0)

    for s in range(STREAMS):
        off, n = OFFSETS[s], COUNTS[s]
        pairs[s].wait_recv()
        add(work, off, 0, grad_ref, mine + off, 0, pair_buf, off, n, D)
        launch(s, 0)

    for k in range(ROUNDS):
        half = 512 >> k
        for s in range(STREAMS):
            off, n = OFFSETS[s], COUNTS[s]
            flying[s].wait_recv()
            if k + 1 < ROUNDS:
                add(work, off, starts[s], work, off, starts[s], bufs[k], off, n, half)
                launch(s, k + 1)
            else:
                add(out_ref, mine + off, starts[s], work, off, starts[s], bufs[k], off, n, half)
                gather(s, k, copy, out_ref, mine, starts, history, ag_s, ag_r, flying, pending)

    handed = []

    def hand(s, part, start):
        span = pl.ds(pl.multiple_of(start, 16), 512)
        slots = pl.ds(mine + OFFSETS[s], COUNTS[s])
        c = copy(
            out_ref.at[slots, span], out_ref.at[slots, span], fin_s.at[part, s], fin_r.at[part, s], partner
        )
        c.start()
        handed.append(c)

    for k in range(ROUNDS - 1, -1, -1):
        half = 512 >> k
        for s in range(STREAMS):
            flying[s].wait_recv()
            _, keep = route(coords, core, s, k)
            before = starts[s]
            starts[s] = before - keep * half
            if k > 0:
                gather(s, k - 1, copy, out_ref, mine, starts, history, ag_s, ag_r, flying, pending)
                if k == 1:
                    hand(s, 0, starts[s])
            else:
                hand(s, 1, 512 - before)
    for c in handed:
        c.wait_recv()
        c.wait_send()
    for s in range(STREAMS):
        pairs[s].wait_send()
    for c in pending:
        c.wait_send()


def gather(s, k, copy, out_ref, mine, starts, history, ag_s, ag_r, flying, pending):
    half = 512 >> k
    slots = pl.ds(mine + OFFSETS[s], COUNTS[s])
    span = pl.ds(pl.multiple_of(starts[s], 16), half)
    c = copy(
        out_ref.at[slots, span], out_ref.at[slots, span], ag_s.at[s, k], ag_r.at[s, k], history[s][k]
    )
    c.start()
    flying[s] = c
    pending.append(c)


def reduce_all(grads):
    dma = pltpu.SemaphoreType.DMA
    return pl.pallas_call(
        reduce_kernel,
        name="reduce_all",
        out_shape=jax.ShapeDtypeStruct((SLABS, D, 128), BF16),
        in_specs=[VM],
        out_specs=VM,
        scratch_shapes=[pltpu.VMEM((OWN, D, 128), BF16)] * 2
        + [pltpu.VMEM((OWN, 512 >> k, 128), BF16) for k in range(ROUNDS)]
        + [dma((STREAMS,))] * 2 + [dma((STREAMS, ROUNDS))] * 4 + [dma((2, STREAMS))] * 2,
        compiler_params=pltpu.CompilerParams(
            collective_id=0, has_side_effects=True, vmem_limit_bytes=48 << 20
        ),
    )(grads)


def finish_kernel(
    in_ref, mid_ref, head_ref, small_ref, loss_ref, g1_ref, g2_ref,
    win_ref, wout_ref, hw_ref, depth_ref, gain1_ref, gain2_ref, utt_ref, scale,
):
    @pl.when(pl.program_id(0) == 0)
    def _():
        first = small_ref[0, 0:16, :].astype(F32)[0:1, :]
        lane = lax.broadcasted_iota(jnp.int32, (1, 128), 1)
        place = jnp.left_shift(1, jnp.clip(lane - 64, 0, 12)).astype(F32)
        used = (lane >= 64) & (lane < 74)
        count = jnp.sum(jnp.where(used, first * place, 0.0), axis=-1, keepdims=True)
        inv = UTTS / count
        scale[...] = jnp.broadcast_to(inv, (8, 128))
        utt_ref[...] = loss_ref[...] * inv
        small = small_ref[0].astype(F32).T * inv
        depth_ref[...] = small[0:TAPS, :]
        gain1_ref[...] = small[32:33, :] / g1_ref[...]
        gain2_ref[...] = small[33:34, :] / g2_ref[...]

    inv = scale[0:1, :]
    for j in range(2):
        win_ref[:, j * 128 : (j + 1) * 128] = in_ref[j].astype(F32) * inv
        hw_ref[:, j * 128 : (j + 1) * 128] = head_ref[j].astype(F32) * inv
    wout_ref[...] = mid_ref[0].astype(F32) * inv


UTTS = 256.0


def finish(total, loss, gain_conv, gain_out):
    sd = jax.ShapeDtypeStruct
    whole = lambda *shape: pl.BlockSpec(shape, lambda i: (0,) * len(shape))
    outs = pl.pallas_call(
        finish_kernel,
        name="finish",
        grid=(8,),
        out_shape=(
            sd((D, 2 * D), F32), sd((D, D), F32), sd((D, V), F32), sd((TAPS, D), F32),
            sd((1, D), F32), sd((1, D), F32), sd((UTT, 128), F32),
        ),
        in_specs=[
            pl.BlockSpec((2, D, 128), lambda i: (i, 0, 0)),
            pl.BlockSpec((1, D, 128), lambda i: (16 + i, 0, 0)),
            pl.BlockSpec((2, 128, 128), lambda i: (12, i, 0)),
            pl.BlockSpec((1, D, 128), lambda i: (26, 0, 0)),
            whole(UTT, 128), whole(1, D), whole(1, D),
        ],
        out_specs=[
            pl.BlockSpec((D, 256), lambda i: (0, i)),
            pl.BlockSpec((D, 128), lambda i: (0, i)),
            pl.BlockSpec((128, V), lambda i: (i, 0)),
            whole(TAPS, D), whole(1, D), whole(1, D), whole(UTT, 128),
        ],
        scratch_shapes=[pltpu.VMEM((8, 128), F32)],
    )(total, total, total, total, loss, gain_conv.reshape(1, D), gain_out.reshape(1, D))
    win, wout, hw, depth, gain1, gain2, utt = outs
    return gain1.reshape(D), win, depth, wout, gain2.reshape(D), hw, utt[:, 0]


def on_device(
    features, teacher_logits, lengths, gain_conv, weight_in, weight_depth, weight_out, gain_out, head_weight
):
    member = lax.axis_index("member")
    give = lax.dynamic_slice_in_dim(teacher_logits, (1 - member) * UTT, UTT, 1)
    own = lax.dynamic_slice_in_dim(teacher_logits, member * UTT, UTT, 1)
    got = lax.ppermute(give, "member", ((0, 1), (1, 0)))
    grads, loss = compute(
        features, own, got, lengths, gain_conv, weight_in, weight_depth, weight_out, gain_out, head_weight
    )
    return finish(reduce_all(grads), loss, gain_conv, gain_out)


def solution(mesh):
    in_specs = (
        P(("dp", "member"), None, None), P("member", "dp", None, None), P(("dp", "member")),
        P(), P(), P(), P(), P(), P(),
    )
    out_specs = (P(), P(), P(), P(), P(), P(), P(("dp", "member")))
    return jax.shard_map(on_device, mesh=mesh, in_specs=in_specs, out_specs=out_specs, check_vma=False)
```

```python
import functools
import math

import jax
import jax.numpy as jnp
import numpy as np
from jax import lax
from jax.experimental import pallas as pl
from jax.experimental.pallas import tpu as pltpu
from jax.sharding import PartitionSpec as P

D, V, TAPS, FRAMES, UTT = 1024, 256, 31, 256, 2
TOK = UTT * FRAMES
PERIOD, HALF, ROWS = 272, 144, 288
TILE = 256
SLABS = 28
OWN = 14
OUT_SLOT, HEAD_SLOT, SMALL_SLOT = 8, 12, 13
F32, BF16 = jnp.float32, jnp.bfloat16
VM = pl.BlockSpec(memory_space=pltpu.VMEM)
SM = pl.BlockSpec(memory_space=pltpu.SMEM)


def transforms():
    freq = np.arange(PERIOD // 2 + 1)
    time = np.arange(FRAMES)
    angle = 2 * np.pi * np.outer(freq, time) / PERIOD
    analysis = np.zeros((ROWS, FRAMES))
    analysis[: freq.size] = np.cos(angle)
    analysis[HALF : HALF + freq.size] = np.sin(angle)
    lag = np.arange(TAPS) - TAPS // 2
    weight = np.where((freq == 0) | (freq == PERIOD // 2), 1.0, 2.0)[:, None] / PERIOD
    turn = 2 * np.pi * np.outer(freq, lag) / PERIOD
    taps = np.zeros((ROWS, TAPS + 1))
    taps[: freq.size, :TAPS] = np.cos(turn) * weight
    taps[HALF : HALF + freq.size, :TAPS] = np.sin(turn) * weight
    lags = np.zeros((ROWS, 128))
    lags[:, : TAPS + 1] = taps
    bf = lambda v: jnp.asarray(v, F32).astype(BF16)
    return bf(analysis), bf(analysis.T), jnp.asarray(taps, F32), bf(lags)


def dot(a, b):
    return jnp.dot(a, b, preferred_element_type=F32)


def dot_bt(a, b):
    return lax.dot_general(a, b, (((1,), (1,)), ((), ())), preferred_element_type=F32)


def dot_at(a, b):
    return lax.dot_general(a, b, (((0,), (0,)), ((), ())), preferred_element_type=F32)


def sigmoid(v):
    return 1.0 / (1.0 + jnp.exp(-v))


def rows_loop(total, step, body):
    def run(i, c):
        body(pl.ds(pl.multiple_of(i * step, step), step), i)
        return c

    lax.fori_loop(0, total // step, run, 0)


def forward_kernel(
    len_ref, x_ref, g1_ref, win_ref, taps_ref, wout_ref, g2_ref, head_ref, tm_ref, c_ref, ct_ref,
    normed_ref, a_ref, s_ref, spec_ref, fac_ref, act_ref, z_ref, rstd_ref, fn_ref, logit_ref,
    taps32, res,
):
    taps32[...] = jnp.zeros_like(taps32)
    taps32[0:TAPS, :] = taps_ref[...]

    def norm_rows(rows, i):
        v = x_ref[rows, :].astype(F32)
        v = v - jnp.mean(v, axis=-1, keepdims=True)
        v = v * lax.rsqrt(jnp.mean(v * v, axis=-1, keepdims=True) + 1e-5)
        normed_ref[rows, :] = (v * g1_ref[...]).astype(BF16)

    rows_loop(TOK, 32, norm_rows)

    def channel_tile(cb, carry):
        cols = pl.ds(pl.multiple_of(cb * TILE, TILE), TILE)
        gate_cols = pl.ds(pl.multiple_of(D + cb * TILE, TILE), TILE)
        hat = jnp.dot(
            tm_ref[...], taps32[:, cols], preferred_element_type=F32, precision=lax.Precision.HIGHEST
        )
        hr, hi = hat[:HALF], hat[HALF:]
        for u in range(UTT):
            rows = pl.ds(u * FRAMES, FRAMES)
            live = lax.broadcasted_iota(jnp.int32, (FRAMES, TILE), 0) < len_ref[u]
            nu = normed_ref[rows, :]
            a = dot(nu, win_ref[:, cols])
            s = sigmoid(dot(nu, win_ref[:, gate_cols]))
            a = jnp.where(live, a, 0.0)
            s_ref[rows, cols] = s.astype(BF16)
            a_ref[rows, cols] = a.astype(BF16)
            sp = dot(c_ref[...], (a * s).astype(BF16))
            spec_ref[u, :, cols] = sp.astype(BF16)
            xr, xi = sp[:HALF], sp[HALF:]
            prod = jnp.concatenate([xr * hr + xi * hi, xi * hr - xr * hi], axis=0)
            conv = dot(ct_ref[...], prod.astype(BF16))
            sg = sigmoid(conv)
            act_ref[rows, cols] = (conv * sg).astype(BF16)
            fac_ref[rows, cols] = (sg * (1.0 + conv * (1.0 - sg))).astype(BF16)
        return carry

    lax.fori_loop(0, D // TILE, channel_tile, 0)

    def out_tile(cb, carry):
        cols = pl.ds(pl.multiple_of(cb * TILE, TILE), TILE)
        res[:, cols] = x_ref[:, cols].astype(F32) + dot(act_ref[...], wout_ref[:, cols])
        return carry

    lax.fori_loop(0, D // TILE, out_tile, 0)

    def norm_out(rows, i):
        v = res[rows, :]
        v = v - jnp.mean(v, axis=-1, keepdims=True)
        r = lax.rsqrt(jnp.mean(v * v, axis=-1, keepdims=True) + 1e-5)
        z = v * r
        z_ref[rows, :] = z.astype(BF16)
        rstd_ref[rows, :] = jnp.broadcast_to(r, (32, 128))
        fn_ref[rows, :] = (z * g2_ref[...]).astype(BF16)

    rows_loop(TOK, 32, norm_out)
    logit_ref[...] = dot(fn_ref[...], head_ref[...])


def softmax_parts(v):
    m = jnp.max(v, axis=-1, keepdims=True)
    e = jnp.exp(v - m)
    return m, e, jnp.sum(e, axis=-1, keepdims=True)


def backward_kernel(
    len_ref, own_ref, got_ref, logit_ref, fn_ref, z_ref, rstd_ref, act_ref, fac_ref, spec_ref, s_ref, a_ref,
    normed_ref, win_ref, taps_ref, wout_ref, g2_ref, head_ref, tm_ref, c_ref, ct_ref, lag_ref,
    grad_ref, loss_ref, pair_ref,
    taps32, dl, dz, dr, dp, gain1, left, pair_s, pair_r,
):
    coords, core = position()
    partner = device(coords, 1 - core)
    theirs = (1 - core) * OWN
    barrier = pltpu.get_barrier_semaphore()
    pl.semaphore_signal(barrier, inc=1, device_id=partner, device_id_type=MESH)

    def handover(slot, n, sem):
        return pltpu.make_async_remote_copy(
            src_ref=grad_ref.at[pl.ds(theirs + slot, n)], dst_ref=pair_ref.at[pl.ds(slot, n)],
            send_sem=pair_s.at[sem], recv_sem=pair_r.at[sem], device_id=partner, device_id_type=MESH,
        )

    taps32[...] = jnp.zeros_like(taps32)
    taps32[0:TAPS, :] = taps_ref[...]
    gain1[...] = jnp.zeros_like(gain1)

    for u in range(UTT):
        length = len_ref[u]

        def loss_rows(i, total):
            rows = pl.ds(pl.multiple_of(i * 32, 32), 32)
            flat = pl.ds(pl.multiple_of(u * FRAMES + i * 32, 32), 32)
            summed = jnp.zeros((32, V), F32)
            for ref in (own_ref, got_ref):
                for k in range(2):
                    t = ref[k, u, rows, :].astype(F32)
                    m, _, z = softmax_parts(t)
                    summed = summed + (t - m - jnp.log(z))
            _, e, z = softmax_parts(summed * 0.25)
            target = e / z
            lg = logit_ref[flat, :]
            m, e, z = softmax_parts(lg)
            live = i * 32 + lax.broadcasted_iota(jnp.int32, (32, V), 0) < length
            ce = jnp.sum(jnp.where(live, target * (m + jnp.log(z) - lg), 0.0), axis=0, keepdims=True)
            mass = jnp.sum(target, axis=-1, keepdims=True)
            dl[flat, :] = jnp.where(live, e * (mass / z) - target, 0.0).astype(BF16)
            return total + ce

        total = lax.fori_loop(0, FRAMES // 32, loss_rows, jnp.zeros((1, V), F32))
        loss_ref[u : u + 1, :] = jnp.broadcast_to(jnp.sum(total, axis=-1, keepdims=True), (1, 128))

    def head_tile(cb, carry):
        cols = pl.ds(pl.multiple_of(cb * TILE, TILE), TILE)
        rows = cols
        dz[:, cols] = dot_bt(dl[...], head_ref[rows, :])
        dh = dot_at(fn_ref[:, cols], dl[...])
        grad_ref[HEAD_SLOT, rows, :] = dh[:, :128].astype(BF16)
        grad_ref[OWN + HEAD_SLOT, rows, :] = dh[:, 128:].astype(BF16)
        left[1, rows, :] = jnp.broadcast_to(
            jnp.sum(dh * head_ref[rows, :].astype(F32), axis=-1, keepdims=True), (TILE, 128)
        )
        return carry

    lax.fori_loop(0, D // TILE, head_tile, 0)
    pl.semaphore_wait(barrier, 1)
    copies = [handover(HEAD_SLOT, 1, 4)]
    copies[0].start()

    def norm_rows(rows, i):
        g = dz[rows, :] * g2_ref[...]
        z = z_ref[rows, :].astype(F32)
        r = rstd_ref[rows, :][:, :1]
        m1 = jnp.mean(g, axis=-1, keepdims=True)
        m2 = jnp.mean(g * z, axis=-1, keepdims=True)
        dr[rows, :] = (r * (g - m1 - z * m2)).astype(BF16)

    rows_loop(TOK, 32, norm_rows)

    def conv_tile(cb, carry):
        cols = pl.ds(pl.multiple_of(cb * TILE, TILE), TILE)
        gate_cols = pl.ds(pl.multiple_of(D + cb * TILE, TILE), TILE)
        hat = jnp.dot(
            tm_ref[...], taps32[:, cols], preferred_element_type=F32, precision=lax.Precision.HIGHEST
        )
        hr, hi = hat[:HALF], hat[HALF:]
        q = jnp.zeros((ROWS, TILE), F32)
        for u in range(UTT):
            rows = pl.ds(u * FRAMES, FRAMES)
            dact = dot_bt(dr[rows, :], wout_ref[cols, :])
            dc = (dact * fac_ref[rows, cols].astype(F32)).astype(BF16)
            sp = dot(c_ref[...], dc)
            er, ei = sp[:HALF], sp[HALF:]
            x = spec_ref[u, :, cols].astype(F32)
            xr, xi = x[:HALF], x[HALF:]
            q = q + jnp.concatenate([er * xr + ei * xi, er * xi - ei * xr], axis=0)
            back = jnp.concatenate([er * hr - ei * hi, ei * hr + er * hi], axis=0)
            dg = dot(ct_ref[...], back.astype(BF16))
            live = lax.broadcasted_iota(jnp.int32, (FRAMES, TILE), 0) < len_ref[u]
            s = s_ref[rows, cols].astype(F32)
            a = a_ref[rows, cols].astype(F32)
            ds = jnp.where(live, dg * s, 0.0)
            dp[rows, cols] = ds.astype(BF16)
            dp[rows, gate_cols] = (ds * a * (1.0 - s)).astype(BF16)
        left[0, cols, :] = dot_at(q.astype(BF16), lag_ref[...])
        dw = dot_at(act_ref[:, cols], dr[...])
        for j in range(8):
            grad_ref[OUT_SLOT + j % 4 + OWN * (j // 4), cols, :] = dw[:, j * 128 : (j + 1) * 128].astype(BF16)
        return carry

    lax.fori_loop(0, D // TILE, conv_tile, 0)
    copies.append(handover(OUT_SLOT, 4, 5))
    copies[1].start()

    def in_tile(group, i):
        n = group * 4 + i
        slot = group * OWN + 2 * i
        cols = pl.ds(pl.multiple_of(n * TILE, TILE), TILE)
        dw = dot_at(normed_ref[...], dp[:, cols])
        grad_ref[slot] = dw[:, :128].astype(BF16)
        grad_ref[slot + 1] = dw[:, 128:].astype(BF16)
        w = dw * win_ref[:, cols].astype(F32)
        gain1[...] += w[:, :128] + w[:, 128:]

    def away(i, carry):
        in_tile(1 - core, i)
        handover(2 * i, 2, i).start()
        return carry

    def home(i, carry):
        in_tile(core, i)
        return carry

    lax.fori_loop(0, 4, away, 0)
    lax.fori_loop(0, 4, home, 0)

    count = len_ref[0] + len_ref[1]

    def small_rows(rows, i):
        lane = lax.broadcasted_iota(jnp.int32, (128, 128), 1)
        bit = jnp.right_shift(count, jnp.clip(lane - 64, 0, 15)) & 1
        g1 = jnp.sum(gain1[rows, :], axis=-1, keepdims=True)
        out = jnp.where(lane < TAPS, left[0, rows, :], 0.0)
        out = jnp.where(lane == 32, g1, out)
        out = jnp.where(lane == 33, left[1, rows, :], out)
        out = jnp.where((lane >= 64) & (lane < 74), bit.astype(F32), out)
        grad_ref[SMALL_SLOT, rows, :] = out.astype(BF16)
        grad_ref[OWN + SMALL_SLOT, rows, :] = jnp.zeros((128, 128), BF16)

    rows_loop(D, 128, small_rows)
    copies.append(handover(SMALL_SLOT, 1, 6))
    copies[2].start()
    for i in range(4):
        copies.append(handover(2 * i, 2, i))
    for c in copies:
        c.wait_recv()
        c.wait_send()


def compute(features, own, got, lengths, gain_conv, weight_in, weight_depth, weight_out, gain_out, head):
    analysis, synthesis, tapm, lagm = transforms()
    sd = jax.ShapeDtypeStruct
    cp = pltpu.CompilerParams(vmem_limit_bytes=60 << 20)
    g1, g2 = gain_conv.reshape(1, D), gain_out.reshape(1, D)
    fwd = pl.pallas_call(
        forward_kernel,
        name="forward",
        out_shape=(
            sd((TOK, D), BF16), sd((TOK, D), BF16), sd((TOK, D), BF16), sd((UTT, ROWS, D), BF16),
            sd((TOK, D), BF16), sd((TOK, D), BF16), sd((TOK, D), BF16), sd((TOK, 128), F32),
            sd((TOK, D), BF16), sd((TOK, V), F32),
        ),
        in_specs=[SM] + [VM] * 10,
        out_specs=[VM] * 10,
        scratch_shapes=[pltpu.VMEM((32, D), F32), pltpu.VMEM((TOK, D), F32)],
        compiler_params=cp,
        cost_estimate=pl.CostEstimate(flops=4 * 10**9, bytes_accessed=20 << 20, transcendentals=2 << 20),
    )
    normed, a, s, spec, fac, act, z, rstd, fn, logit = fwd(
        lengths, features.reshape(TOK, D), g1, weight_in, weight_depth, weight_out, g2, head,
        tapm, analysis, synthesis,
    )
    bwd = pl.pallas_call(
        backward_kernel,
        name="backward",
        out_shape=(sd((SLABS, D, 128), BF16), sd((UTT, 128), F32), sd((OWN, D, 128), BF16)),
        in_specs=[SM] + [VM] * 21,
        out_specs=[VM] * 3,
        scratch_shapes=[
            pltpu.VMEM((32, D), F32), pltpu.VMEM((TOK, V), BF16), pltpu.VMEM((TOK, D), F32),
            pltpu.VMEM((TOK, D), BF16), pltpu.VMEM((TOK, 2 * D), BF16), pltpu.VMEM((D, 128), F32),
            pltpu.VMEM((2, D, 128), F32), pltpu.SemaphoreType.DMA((7,)), pltpu.SemaphoreType.DMA((7,)),
        ],
        compiler_params=pltpu.CompilerParams(
            collective_id=1, has_side_effects=True, vmem_limit_bytes=60 << 20
        ),
    )
    return bwd(
        lengths, own, got, logit, fn, z, rstd, act, fac, spec, s, a, normed, weight_in, weight_depth,
        weight_out, g2, head, tapm, analysis, synthesis, lagm,
    )


MESH = pl.DeviceIdType.MESH
STREAMS = 12
COUNTS = (2, 1, 1, 1, 1, 1, 1, 2, 1, 1, 1, 1)
OFFSETS = (0, 2, 3, 4, 5, 6, 7, 8, 10, 11, 12, 13)
ROUNDS = 6


def position():
    member, dp = lax.axis_index("member"), lax.axis_index("dp")
    core, z, rest = dp % 2, (dp // 2) % 4, dp // 8
    return ((rest % 2) * 2 + member, rest // 2, z), core


def device(coords, core):
    x, y, z = coords
    return {"member": x % 2, "dp": ((y * 2 + x // 2) * 4 + z) * 2 + core}


def other(c, wide):
    return 3 - c if wide else c + 1 - 2 * (c % 2)


def kept(c, kind, second):
    if kind == 0 and not second:
        return (c + c // 2) % 2
    return c % 2 if (kind == 1 and second) else c // 2


def route(coords, core, s, k):
    s = s % 6
    dim = (s // 2 + core + k // 2) % 3
    hit = [jnp.where(dim == d, 1, 0) for d in range(3)]
    c = sum(h * v for h, v in zip(hit, coords))
    kind, second = s % 2, k % 2
    p = other(c, (kind + second) % 2 == 1)
    peer = [v + h * (p - v) for h, v in zip(hit, coords)]
    return device(peer, core), kept(c, kind, second == 1)


def reduce_kernel(
    grad_ref, pair_buf, out_ref, work, *rest
):
    bufs = rest[:ROUNDS]
    rs_s, rs_r, ag_s, ag_r, fin_s, fin_r = rest[ROUNDS:]
    coords, core = position()
    partner = device(coords, 1 - core)
    mine = core * OWN

    barrier = pltpu.get_barrier_semaphore()
    greet = [partner]
    for d in range(3):
        for wide in (False, True):
            greet.append(device([other(v, wide) if i == d else v for i, v in enumerate(coords)], core))
    for dev in greet:
        pl.semaphore_signal(barrier, inc=1, device_id=dev, device_id_type=MESH)

    def copy(src, dst, send, recv, dev):
        return pltpu.make_async_remote_copy(
            src_ref=src, dst_ref=dst, send_sem=send, recv_sem=recv, device_id=dev, device_id_type=MESH
        )

    pending = []

    starts = [jnp.int32(0)] * STREAMS
    history = [[] for _ in range(STREAMS)]
    flying = [None] * STREAMS

    def launch(s, k):
        half = 512 >> k
        dev, keep = route(coords, core, s, k)
        slots = pl.ds(OFFSETS[s], COUNTS[s])
        give = pl.multiple_of(starts[s] + (1 - keep) * half, 16)
        c = copy(
            work.at[slots, pl.ds(give, half)],
            bufs[k].at[pl.ds(OFFSETS[s], COUNTS[s])],
            rs_s.at[s, k], rs_r.at[s, k], dev,
        )
        c.start()
        flying[s] = c
        pending.append(c)
        starts[s] = starts[s] + keep * half
        history[s].append(dev)

    def add(dst_ref, dst_slot, dst_row, a_ref, a_slot, a_row, b_ref, b_slot, n, size):
        step = min(size, 128)

        def run(i, carry):
            r = i * step
            for j in range(n):
                d = pl.ds(pl.multiple_of(dst_row + r, 16), step)
                a = a_ref[a_slot + j, pl.ds(pl.multiple_of(a_row + r, 16), step), :]
                b = b_ref[b_slot + j, pl.ds(pl.multiple_of(r, 16), step), :]
                dst_ref[dst_slot + j, d, :] = a + b
            return carry

        lax.fori_loop(0, size // step, run, 0)

    for s in range(STREAMS):
        off, n = OFFSETS[s], COUNTS[s]
        add(work, off, 0, grad_ref, mine + off, 0, pair_buf, off, n, D)
        if s == 0:
            pl.semaphore_wait(barrier, len(greet))
        launch(s, 0)

    for k in range(ROUNDS):
        half = 512 >> k
        for s in range(STREAMS):
            off, n = OFFSETS[s], COUNTS[s]
            flying[s].wait_recv()
            if k + 1 < ROUNDS:
                add(work, off, starts[s], work, off, starts[s], bufs[k], off, n, half)
                launch(s, k + 1)
            else:
                add(out_ref, mine + off, starts[s], work, off, starts[s], bufs[k], off, n, half)
                gather(s, k, copy, out_ref, mine, starts, history, ag_s, ag_r, flying, pending)

    handed = []

    def hand(s, part, start):
        span = pl.ds(pl.multiple_of(start, 16), 512)
        slots = pl.ds(mine + OFFSETS[s], COUNTS[s])
        c = copy(
            out_ref.at[slots, span], out_ref.at[slots, span], fin_s.at[part, s], fin_r.at[part, s], partner
        )
        c.start()
        handed.append(c)

    for k in range(ROUNDS - 1, -1, -1):
        half = 512 >> k
        for s in range(STREAMS):
            flying[s].wait_recv()
            _, keep = route(coords, core, s, k)
            before = starts[s]
            starts[s] = before - keep * half
            if k > 0:
                gather(s, k - 1, copy, out_ref, mine, starts, history, ag_s, ag_r, flying, pending)
                if k == 1:
                    hand(s, 0, starts[s])
            else:
                hand(s, 1, 512 - before)
    for c in handed:
        c.wait_recv()
        c.wait_send()
    for c in pending:
        c.wait_send()


def gather(s, k, copy, out_ref, mine, starts, history, ag_s, ag_r, flying, pending):
    half = 512 >> k
    slots = pl.ds(mine + OFFSETS[s], COUNTS[s])
    span = pl.ds(pl.multiple_of(starts[s], 16), half)
    c = copy(
        out_ref.at[slots, span], out_ref.at[slots, span], ag_s.at[s, k], ag_r.at[s, k], history[s][k]
    )
    c.start()
    flying[s] = c
    pending.append(c)


def reduce_all(grads, pair):
    dma = pltpu.SemaphoreType.DMA
    return pl.pallas_call(
        reduce_kernel,
        name="reduce_all",
        out_shape=jax.ShapeDtypeStruct((SLABS, D, 128), BF16),
        in_specs=[VM, VM],
        out_specs=VM,
        scratch_shapes=[pltpu.VMEM((OWN, D, 128), BF16)]
        + [pltpu.VMEM((OWN, 512 >> k, 128), BF16) for k in range(ROUNDS)]
        + [dma((STREAMS, ROUNDS))] * 4 + [dma((2, STREAMS))] * 2,
        compiler_params=pltpu.CompilerParams(
            collective_id=0, has_side_effects=True, vmem_limit_bytes=48 << 20
        ),
    )(grads, pair)


def finish_kernel(
    in_ref, mid_ref, left_ref, right_ref, small_ref, loss_ref, g1_ref, g2_ref,
    win_ref, wout_ref, hw_ref, depth_ref, gain1_ref, gain2_ref, utt_ref, scale,
):
    @pl.when(pl.program_id(0) == 0)
    def _():
        first = small_ref[0, 0:16, :].astype(F32)[0:1, :]
        lane = lax.broadcasted_iota(jnp.int32, (1, 128), 1)
        place = jnp.left_shift(1, jnp.clip(lane - 64, 0, 12)).astype(F32)
        used = (lane >= 64) & (lane < 74)
        count = jnp.sum(jnp.where(used, first * place, 0.0), axis=-1, keepdims=True)
        inv = UTTS / count
        scale[...] = jnp.broadcast_to(inv, (8, 128))
        utt_ref[...] = loss_ref[...] * inv
        small = small_ref[0].astype(F32).T * inv
        depth_ref[...] = small[0:TAPS, :]
        gain1_ref[...] = small[32:33, :] / g1_ref[...]
        gain2_ref[...] = small[33:34, :] / g2_ref[...]

    inv = scale[0:1, :]
    for j in range(2):
        win_ref[:, j * 128 : (j + 1) * 128] = in_ref[j].astype(F32) * inv
        head = (left_ref, right_ref)[j]
        hw_ref[:, j * 128 : (j + 1) * 128] = head[0].astype(F32) * inv
    wout_ref[...] = mid_ref[0].astype(F32) * inv


UTTS = 256.0


def finish(total, loss, gain_conv, gain_out):
    sd = jax.ShapeDtypeStruct
    whole = lambda *shape: pl.BlockSpec(shape, lambda i: (0,) * len(shape))
    outs = pl.pallas_call(
        finish_kernel,
        name="finish",
        grid=(8,),
        out_shape=(
            sd((D, 2 * D), F32), sd((D, D), F32), sd((D, V), F32), sd((TAPS, D), F32),
            sd((1, D), F32), sd((1, D), F32), sd((UTT, 128), F32),
        ),
        in_specs=[
            pl.BlockSpec((2, D, 128), lambda i: (i + 3 * (i // 4), 0, 0)),
            pl.BlockSpec((1, D, 128), lambda i: (OUT_SLOT + i + 10 * (i // 4), 0, 0)),
            pl.BlockSpec((1, 128, 128), lambda i: (HEAD_SLOT, i, 0)),
            pl.BlockSpec((1, 128, 128), lambda i: (OWN + HEAD_SLOT, i, 0)),
            pl.BlockSpec((1, D, 128), lambda i: (SMALL_SLOT, 0, 0)),
            whole(UTT, 128), whole(1, D), whole(1, D),
        ],
        out_specs=[
            pl.BlockSpec((D, 256), lambda i: (0, i)),
            pl.BlockSpec((D, 128), lambda i: (0, i)),
            pl.BlockSpec((128, V), lambda i: (i, 0)),
            whole(TAPS, D), whole(1, D), whole(1, D), whole(UTT, 128),
        ],
        scratch_shapes=[pltpu.VMEM((8, 128), F32)],
    )(total, total, total, total, total, loss, gain_conv.reshape(1, D), gain_out.reshape(1, D))
    win, wout, hw, depth, gain1, gain2, utt = outs
    return gain1.reshape(D), win, depth, wout, gain2.reshape(D), hw, utt[:, 0]


def on_device(
    features, teacher_logits, lengths, gain_conv, weight_in, weight_depth, weight_out, gain_out, head_weight
):
    member = lax.axis_index("member")
    give = lax.dynamic_slice_in_dim(teacher_logits, (1 - member) * UTT, UTT, 1)
    own = lax.dynamic_slice_in_dim(teacher_logits, member * UTT, UTT, 1)
    got = lax.ppermute(give, "member", ((0, 1), (1, 0)))
    grads, loss, pair = compute(
        features, own, got, lengths, gain_conv, weight_in, weight_depth, weight_out, gain_out, head_weight
    )
    return finish(reduce_all(grads, pair), loss, gain_conv, gain_out)


def solution(mesh):
    in_specs = (
        P(("dp", "member"), None, None), P("member", "dp", None, None), P(("dp", "member")),
        P(), P(), P(), P(), P(), P(),
    )
    out_specs = (P(), P(), P(), P(), P(), P(), P(("dp", "member")))
    return jax.shard_map(on_device, mesh=mesh, in_specs=in_specs, out_specs=out_specs, check_vma=False)
```

```python
import functools
import math

import jax
import jax.numpy as jnp
import numpy as np
from jax import lax
from jax.experimental import pallas as pl
from jax.experimental.pallas import tpu as pltpu
from jax.sharding import PartitionSpec as P

D, V, TAPS, FRAMES, UTT = 1024, 256, 31, 256, 2
TOK = UTT * FRAMES
PERIOD, HALF, ROWS = 272, 144, 288
TILE = 256
SLABS = 28
F32, BF16 = jnp.float32, jnp.bfloat16
VM = pl.BlockSpec(memory_space=pltpu.VMEM)
SM = pl.BlockSpec(memory_space=pltpu.SMEM)


def transforms():
    freq = np.arange(PERIOD // 2 + 1)
    time = np.arange(FRAMES)
    angle = 2 * np.pi * np.outer(freq, time) / PERIOD
    analysis = np.zeros((ROWS, FRAMES))
    analysis[: freq.size] = np.cos(angle)
    analysis[HALF : HALF + freq.size] = np.sin(angle)
    lag = np.arange(TAPS) - TAPS // 2
    weight = np.where((freq == 0) | (freq == PERIOD // 2), 1.0, 2.0)[:, None] / PERIOD
    turn = 2 * np.pi * np.outer(freq, lag) / PERIOD
    taps = np.zeros((ROWS, TAPS + 1))
    taps[: freq.size, :TAPS] = np.cos(turn) * weight
    taps[HALF : HALF + freq.size, :TAPS] = np.sin(turn) * weight
    lags = np.zeros((ROWS, 128))
    lags[:, : TAPS + 1] = taps
    bf = lambda v: jnp.asarray(v, F32).astype(BF16)
    return bf(analysis), bf(analysis.T), jnp.asarray(taps, F32), bf(lags)


def dot(a, b):
    return jnp.dot(a, b, preferred_element_type=F32)


def dot_bt(a, b):
    return lax.dot_general(a, b, (((1,), (1,)), ((), ())), preferred_element_type=F32)


def dot_at(a, b):
    return lax.dot_general(a, b, (((0,), (0,)), ((), ())), preferred_element_type=F32)


def sigmoid(v):
    return 1.0 / (1.0 + jnp.exp(-v))


def rows_loop(total, step, body):
    def run(i, c):
        body(pl.ds(pl.multiple_of(i * step, step), step), i)
        return c

    lax.fori_loop(0, total // step, run, 0)


def forward_kernel(
    len_ref, x_ref, g1_ref, win_ref, taps_ref, wout_ref, g2_ref, head_ref, tm_ref, c_ref, ct_ref,
    normed_ref, a_ref, s_ref, spec_ref, fac_ref, act_ref, z_ref, rstd_ref, fn_ref, logit_ref,
    taps32, res,
):
    taps32[...] = jnp.zeros_like(taps32)
    taps32[0:TAPS, :] = taps_ref[...]

    def norm_rows(rows, i):
        v = x_ref[rows, :].astype(F32)
        v = v - jnp.mean(v, axis=-1, keepdims=True)
        v = v * lax.rsqrt(jnp.mean(v * v, axis=-1, keepdims=True) + 1e-5)
        normed_ref[rows, :] = (v * g1_ref[...]).astype(BF16)

    rows_loop(TOK, 32, norm_rows)

    def channel_tile(cb, carry):
        cols = pl.ds(pl.multiple_of(cb * TILE, TILE), TILE)
        gate_cols = pl.ds(pl.multiple_of(D + cb * TILE, TILE), TILE)
        hat = jnp.dot(
            tm_ref[...], taps32[:, cols], preferred_element_type=F32, precision=lax.Precision.HIGHEST
        )
        hr, hi = hat[:HALF], hat[HALF:]
        for u in range(UTT):
            rows = pl.ds(u * FRAMES, FRAMES)
            live = lax.broadcasted_iota(jnp.int32, (FRAMES, TILE), 0) < len_ref[u]
            nu = normed_ref[rows, :]
            a = dot(nu, win_ref[:, cols])
            s = sigmoid(dot(nu, win_ref[:, gate_cols]))
            a = jnp.where(live, a, 0.0)
            s_ref[rows, cols] = s.astype(BF16)
            a_ref[rows, cols] = a.astype(BF16)
            sp = dot(c_ref[...], (a * s).astype(BF16))
            spec_ref[u, :, cols] = sp.astype(BF16)
            xr, xi = sp[:HALF], sp[HALF:]
            prod = jnp.concatenate([xr * hr + xi * hi, xi * hr - xr * hi], axis=0)
            conv = dot(ct_ref[...], prod.astype(BF16))
            sg = sigmoid(conv)
            act_ref[rows, cols] = (conv * sg).astype(BF16)
            fac_ref[rows, cols] = (sg * (1.0 + conv * (1.0 - sg))).astype(BF16)
        return carry

    lax.fori_loop(0, D // TILE, channel_tile, 0)

    def out_tile(cb, carry):
        cols = pl.ds(pl.multiple_of(cb * TILE, TILE), TILE)
        res[:, cols] = x_ref[:, cols].astype(F32) + dot(act_ref[...], wout_ref[:, cols])
        return carry

    lax.fori_loop(0, D // TILE, out_tile, 0)

    def norm_out(rows, i):
        v = res[rows, :]
        v = v - jnp.mean(v, axis=-1, keepdims=True)
        r = lax.rsqrt(jnp.mean(v * v, axis=-1, keepdims=True) + 1e-5)
        z = v * r
        z_ref[rows, :] = z.astype(BF16)
        rstd_ref[rows, :] = jnp.broadcast_to(r, (32, 128))
        fn_ref[rows, :] = (z * g2_ref[...]).astype(BF16)

    rows_loop(TOK, 32, norm_out)
    logit_ref[...] = dot(fn_ref[...], head_ref[...])


def softmax_parts(v):
    m = jnp.max(v, axis=-1, keepdims=True)
    e = jnp.exp(v - m)
    return m, e, jnp.sum(e, axis=-1, keepdims=True)


def backward_kernel(
    len_ref, own_ref, got_ref, logit_ref, fn_ref, z_ref, rstd_ref, act_ref, fac_ref, spec_ref, s_ref, a_ref,
    normed_ref, win_ref, taps_ref, wout_ref, g2_ref, head_ref, tm_ref, c_ref, ct_ref, lag_ref,
    grad_ref, loss_ref,
    taps32, dl, dz, dr, dp, gain1, left,
):
    taps32[...] = jnp.zeros_like(taps32)
    taps32[0:TAPS, :] = taps_ref[...]
    gain1[...] = jnp.zeros_like(gain1)
    first = lax.axis_index("member") * UTT

    for u in range(UTT):
        length = len_ref[u]

        def loss_rows(i, total):
            rows = pl.ds(pl.multiple_of(i * 32, 32), 32)
            flat = pl.ds(pl.multiple_of(u * FRAMES + i * 32, 32), 32)
            summed = jnp.zeros((32, V), F32)
            for ref in (own_ref, got_ref):
                for k in range(2):
                    t = ref[k, first + u, rows, :].astype(F32)
                    m, _, z = softmax_parts(t)
                    summed = summed + (t - m - jnp.log(z))
            _, e, z = softmax_parts(summed * 0.25)
            target = e / z
            lg = logit_ref[flat, :]
            m, e, z = softmax_parts(lg)
            live = i * 32 + lax.broadcasted_iota(jnp.int32, (32, V), 0) < length
            ce = jnp.sum(jnp.where(live, target * (m + jnp.log(z) - lg), 0.0), axis=0, keepdims=True)
            mass = jnp.sum(target, axis=-1, keepdims=True)
            dl[flat, :] = jnp.where(live, e * (mass / z) - target, 0.0).astype(BF16)
            return total + ce

        total = lax.fori_loop(0, FRAMES // 32, loss_rows, jnp.zeros((1, V), F32))
        loss_ref[u : u + 1, :] = jnp.broadcast_to(jnp.sum(total, axis=-1, keepdims=True), (1, 128))

    def head_tile(cb, carry):
        cols = pl.ds(pl.multiple_of(cb * TILE, TILE), TILE)
        rows = cols
        dz[:, cols] = dot_bt(dl[...], head_ref[rows, :])
        dh = dot_at(fn_ref[:, cols], dl[...])
        grad_ref[24, rows, :] = dh[:, :128].astype(BF16)
        grad_ref[25, rows, :] = dh[:, 128:].astype(BF16)
        left[1, rows, :] = jnp.broadcast_to(
            jnp.sum(dh * head_ref[rows, :].astype(F32), axis=-1, keepdims=True), (TILE, 128)
        )
        return carry

    lax.fori_loop(0, D // TILE, head_tile, 0)

    def norm_rows(rows, i):
        g = dz[rows, :] * g2_ref[...]
        z = z_ref[rows, :].astype(F32)
        r = rstd_ref[rows, :][:, :1]
        m1 = jnp.mean(g, axis=-1, keepdims=True)
        m2 = jnp.mean(g * z, axis=-1, keepdims=True)
        dr[rows, :] = (r * (g - m1 - z * m2)).astype(BF16)

    rows_loop(TOK, 32, norm_rows)

    def conv_tile(cb, carry):
        cols = pl.ds(pl.multiple_of(cb * TILE, TILE), TILE)
        gate_cols = pl.ds(pl.multiple_of(D + cb * TILE, TILE), TILE)
        hat = jnp.dot(
            tm_ref[...], taps32[:, cols], preferred_element_type=F32, precision=lax.Precision.HIGHEST
        )
        hr, hi = hat[:HALF], hat[HALF:]
        q = jnp.zeros((ROWS, TILE), F32)
        for u in range(UTT):
            rows = pl.ds(u * FRAMES, FRAMES)
            dact = dot_bt(dr[rows, :], wout_ref[cols, :])
            dc = (dact * fac_ref[rows, cols].astype(F32)).astype(BF16)
            sp = dot(c_ref[...], dc)
            er, ei = sp[:HALF], sp[HALF:]
            x = spec_ref[u, :, cols].astype(F32)
            xr, xi = x[:HALF], x[HALF:]
            q = q + jnp.concatenate([er * xr + ei * xi, er * xi - ei * xr], axis=0)
            back = jnp.concatenate([er * hr - ei * hi, ei * hr + er * hi], axis=0)
            dg = dot(ct_ref[...], back.astype(BF16))
            live = lax.broadcasted_iota(jnp.int32, (FRAMES, TILE), 0) < len_ref[u]
            s = s_ref[rows, cols].astype(F32)
            a = a_ref[rows, cols].astype(F32)
            ds = jnp.where(live, dg * s, 0.0)
            dp[rows, cols] = ds.astype(BF16)
            dp[rows, gate_cols] = (ds * a * (1.0 - s)).astype(BF16)
        left[0, cols, :] = dot_at(q.astype(BF16), lag_ref[...])
        dw = dot_at(act_ref[:, cols], dr[...])
        for j in range(8):
            grad_ref[16 + j, cols, :] = dw[:, j * 128 : (j + 1) * 128].astype(BF16)
        return carry

    lax.fori_loop(0, D // TILE, conv_tile, 0)

    def in_tile(n, carry):
        cols = pl.ds(pl.multiple_of(n * TILE, TILE), TILE)
        dw = dot_at(normed_ref[...], dp[:, cols])
        grad_ref[2 * n] = dw[:, :128].astype(BF16)
        grad_ref[2 * n + 1] = dw[:, 128:].astype(BF16)
        w = dw * win_ref[:, cols].astype(F32)
        gain1[...] += w[:, :128] + w[:, 128:]
        return carry

    lax.fori_loop(0, 2 * D // TILE, in_tile, 0)

    count = len_ref[0] + len_ref[1]

    def small_rows(rows, i):
        lane = lax.broadcasted_iota(jnp.int32, (128, 128), 1)
        bit = jnp.right_shift(count, jnp.clip(lane - 64, 0, 15)) & 1
        g1 = jnp.sum(gain1[rows, :], axis=-1, keepdims=True)
        out = jnp.where(lane < TAPS, left[0, rows, :], 0.0)
        out = jnp.where(lane == 32, g1, out)
        out = jnp.where(lane == 33, left[1, rows, :], out)
        out = jnp.where((lane >= 64) & (lane < 74), bit.astype(F32), out)
        grad_ref[26, rows, :] = out.astype(BF16)
        grad_ref[27, rows, :] = jnp.zeros((128, 128), BF16)

    rows_loop(D, 128, small_rows)


def compute(features, own, got, lengths, gain_conv, weight_in, weight_depth, weight_out, gain_out, head):
    analysis, synthesis, tapm, lagm = transforms()
    sd = jax.ShapeDtypeStruct
    cp = pltpu.CompilerParams(vmem_limit_bytes=60 << 20)
    g1, g2 = gain_conv.reshape(1, D), gain_out.reshape(1, D)
    fwd = pl.pallas_call(
        forward_kernel,
        name="forward",
        out_shape=(
            sd((TOK, D), BF16), sd((TOK, D), BF16), sd((TOK, D), BF16), sd((UTT, ROWS, D), BF16),
            sd((TOK, D), BF16), sd((TOK, D), BF16), sd((TOK, D), BF16), sd((TOK, 128), F32),
            sd((TOK, D), BF16), sd((TOK, V), F32),
        ),
        in_specs=[SM] + [VM] * 10,
        out_specs=[VM] * 10,
        scratch_shapes=[pltpu.VMEM((32, D), F32), pltpu.VMEM((TOK, D), F32)],
        compiler_params=cp,
        cost_estimate=pl.CostEstimate(flops=4 * 10**9, bytes_accessed=20 << 20, transcendentals=2 << 20),
    )
    normed, a, s, spec, fac, act, z, rstd, fn, logit = fwd(
        lengths, features.reshape(TOK, D), g1, weight_in, weight_depth, weight_out, g2, head,
        tapm, analysis, synthesis,
    )
    bwd = pl.pallas_call(
        backward_kernel,
        name="backward",
        out_shape=(sd((SLABS, D, 128), BF16), sd((UTT, 128), F32)),
        in_specs=[SM] + [VM] * 21,
        out_specs=[VM] * 2,
        scratch_shapes=[
            pltpu.VMEM((32, D), F32), pltpu.VMEM((TOK, V), BF16), pltpu.VMEM((TOK, D), F32),
            pltpu.VMEM((TOK, D), BF16), pltpu.VMEM((TOK, 2 * D), BF16), pltpu.VMEM((D, 128), F32),
            pltpu.VMEM((2, D, 128), F32),
        ],
        compiler_params=cp,
    )
    return bwd(
        lengths, own, got, logit, fn, z, rstd, act, fac, spec, s, a, normed, weight_in, weight_depth,
        weight_out, g2, head, tapm, analysis, synthesis, lagm,
    )


MESH = pl.DeviceIdType.MESH
STREAMS = 12
COUNTS = (2, 1, 1, 1, 1, 1, 1, 2, 1, 1, 1, 1)
OFFSETS = (0, 2, 3, 4, 5, 6, 7, 8, 10, 11, 12, 13)
OWN = 14
ROUNDS = 6


def position():
    member, dp = lax.axis_index("member"), lax.axis_index("dp")
    core, z, rest = dp % 2, (dp // 2) % 4, dp // 8
    return ((rest % 2) * 2 + member, rest // 2, z), core


def device(coords, core):
    x, y, z = coords
    return {"member": x % 2, "dp": ((y * 2 + x // 2) * 4 + z) * 2 + core}


def other(c, wide):
    return 3 - c if wide else c + 1 - 2 * (c % 2)


def kept(c, kind, second):
    if kind == 0 and not second:
        return (c + c // 2) % 2
    return c % 2 if (kind == 1 and second) else c // 2


def route(coords, core, s, k):
    s = s % 6
    dim = (s // 2 + core + k // 2) % 3
    hit = [jnp.where(dim == d, 1, 0) for d in range(3)]
    c = sum(h * v for h, v in zip(hit, coords))
    kind, second = s % 2, k % 2
    p = other(c, (kind + second) % 2 == 1)
    peer = [v + h * (p - v) for h, v in zip(hit, coords)]
    return device(peer, core), kept(c, kind, second == 1)


def reduce_kernel(
    grad_ref, out_ref, pair_buf, work, *rest
):
    bufs = rest[:ROUNDS]
    pair_s, pair_r, rs_s, rs_r, ag_s, ag_r, fin_s, fin_r = rest[ROUNDS:]
    coords, core = position()
    partner = device(coords, 1 - core)
    mine = core * OWN
    theirs = (1 - core) * OWN

    barrier = pltpu.get_barrier_semaphore()
    greet = [partner]
    for d in range(3):
        for wide in (False, True):
            greet.append(device([other(v, wide) if i == d else v for i, v in enumerate(coords)], core))
    for dev in greet:
        pl.semaphore_signal(barrier, inc=1, device_id=dev, device_id_type=MESH)
    pl.semaphore_wait(barrier, len(greet))

    def copy(src, dst, send, recv, dev):
        return pltpu.make_async_remote_copy(
            src_ref=src, dst_ref=dst, send_sem=send, recv_sem=recv, device_id=dev, device_id_type=MESH
        )

    pending = []
    pairs = []
    for s in range(STREAMS):
        off, n = OFFSETS[s], COUNTS[s]
        c = copy(
            grad_ref.at[pl.ds(theirs + off, n)], pair_buf.at[pl.ds(off, n)], pair_s.at[s], pair_r.at[s], partner
        )
        c.start()
        pairs.append(c)

    starts = [jnp.int32(0)] * STREAMS
    history = [[] for _ in range(STREAMS)]
    flying = [None] * STREAMS

    def launch(s, k):
        half = 512 >> k
        dev, keep = route(coords, core, s, k)
        slots = pl.ds(OFFSETS[s], COUNTS[s])
        give = pl.multiple_of(starts[s] + (1 - keep) * half, 16)
        c = copy(
            work.at[slots, pl.ds(give, half)],
            bufs[k].at[pl.ds(OFFSETS[s], COUNTS[s])],
            rs_s.at[s, k], rs_r.at[s, k], dev,
        )
        c.start()
        flying[s] = c
        pending.append(c)
        starts[s] = starts[s] + keep * half
        history[s].append(dev)

    def add(dst_ref, dst_slot, dst_row, a_ref, a_slot, a_row, b_ref, b_slot, n, size):
        step = min(size, 128)

        def run(i, carry):
            r = i * step
            for j in range(n):
                d = pl.ds(pl.multiple_of(dst_row + r, 16), step)
                a = a_ref[a_slot + j, pl.ds(pl.multiple_of(a_row + r, 16), step), :]
                b = b_ref[b_slot + j, pl.ds(pl.multiple_of(r, 16), step), :]
                dst_ref[dst_slot + j, d, :] = a + b
            return carry

        lax.fori_loop(0, size // step, run, 0)

    for s in range(STREAMS):
        off, n = OFFSETS[s], COUNTS[s]
        pairs[s].wait_recv()
        add(work, off, 0, grad_ref, mine + off, 0, pair_buf, off, n, D)
        launch(s, 0)

    for k in range(ROUNDS):
        half = 512 >> k
        for s in range(STREAMS):
            off, n = OFFSETS[s], COUNTS[s]
            flying[s].wait_recv()
            if k + 1 < ROUNDS:
                add(work, off, starts[s], work, off, starts[s], bufs[k], off, n, half)
                launch(s, k + 1)
            else:
                add(out_ref, mine + off, starts[s], work, off, starts[s], bufs[k], off, n, half)
                gather(s, k, copy, out_ref, mine, starts, history, ag_s, ag_r, flying, pending)

    handed = []

    def hand(s, part, start):
        span = pl.ds(pl.multiple_of(start, 16), 512)
        slots = pl.ds(mine + OFFSETS[s], COUNTS[s])
        c = copy(
            out_ref.at[slots, span], out_ref.at[slots, span], fin_s.at[part, s], fin_r.at[part, s], partner
        )
        c.start()
        handed.append(c)

    for k in range(ROUNDS - 1, -1, -1):
        half = 512 >> k
        for s in range(STREAMS):
            flying[s].wait_recv()
            _, keep = route(coords, core, s, k)
            before = starts[s]
            starts[s] = before - keep * half
            if k > 0:
                gather(s, k - 1, copy, out_ref, mine, starts, history, ag_s, ag_r, flying, pending)
                if k == 1:
                    hand(s, 0, starts[s])
            else:
                hand(s, 1, 512 - before)
    for c in handed:
        c.wait_recv()
        c.wait_send()
    for s in range(STREAMS):
        pairs[s].wait_send()
    for c in pending:
        c.wait_send()


def gather(s, k, copy, out_ref, mine, starts, history, ag_s, ag_r, flying, pending):
    half = 512 >> k
    slots = pl.ds(mine + OFFSETS[s], COUNTS[s])
    span = pl.ds(pl.multiple_of(starts[s], 16), half)
    c = copy(
        out_ref.at[slots, span], out_ref.at[slots, span], ag_s.at[s, k], ag_r.at[s, k], history[s][k]
    )
    c.start()
    flying[s] = c
    pending.append(c)


def reduce_all(grads):
    dma = pltpu.SemaphoreType.DMA
    return pl.pallas_call(
        reduce_kernel,
        name="reduce_all",
        out_shape=jax.ShapeDtypeStruct((SLABS, D, 128), BF16),
        in_specs=[VM],
        out_specs=VM,
        scratch_shapes=[pltpu.VMEM((OWN, D, 128), BF16)] * 2
        + [pltpu.VMEM((OWN, 512 >> k, 128), BF16) for k in range(ROUNDS)]
        + [dma((STREAMS,))] * 2 + [dma((STREAMS, ROUNDS))] * 4 + [dma((2, STREAMS))] * 2,
        compiler_params=pltpu.CompilerParams(
            collective_id=0, has_side_effects=True, vmem_limit_bytes=48 << 20
        ),
    )(grads)


def finish_kernel(
    in_ref, mid_ref, head_ref, small_ref, loss_ref, g1_ref, g2_ref,
    win_ref, wout_ref, hw_ref, depth_ref, gain1_ref, gain2_ref, utt_ref, scale,
):
    @pl.when(pl.program_id(0) == 0)
    def _():
        first = small_ref[0, 0:16, :].astype(F32)[0:1, :]
        lane = lax.broadcasted_iota(jnp.int32, (1, 128), 1)
        place = jnp.left_shift(1, jnp.clip(lane - 64, 0, 12)).astype(F32)
        used = (lane >= 64) & (lane < 74)
        count = jnp.sum(jnp.where(used, first * place, 0.0), axis=-1, keepdims=True)
        inv = UTTS / count
        scale[...] = jnp.broadcast_to(inv, (8, 128))
        for u in range(UTT):
            utt_ref[u] = jnp.max(loss_ref[u : u + 1, :] * inv)
        small = small_ref[0].astype(F32).T * inv
        depth_ref[...] = small[0:TAPS, :]
        gain1_ref[...] = small[32:33, :] / g1_ref[...]
        gain2_ref[...] = small[33:34, :] / g2_ref[...]

    inv = scale[0:1, :]
    for j in range(2):
        win_ref[:, j * 128 : (j + 1) * 128] = in_ref[j].astype(F32) * inv
        hw_ref[:, j * 128 : (j + 1) * 128] = head_ref[j].astype(F32) * inv
    wout_ref[...] = mid_ref[0].astype(F32) * inv


UTTS = 256.0


def finish(total, loss, gain_conv, gain_out):
    sd = jax.ShapeDtypeStruct
    whole = lambda *shape: pl.BlockSpec(shape, lambda i: (0,) * len(shape))
    outs = pl.pallas_call(
        finish_kernel,
        name="finish",
        grid=(8,),
        out_shape=(
            sd((D, 2 * D), F32), sd((D, D), F32), sd((D, V), F32), sd((TAPS, D), F32),
            sd((1, D), F32), sd((1, D), F32), sd((UTT,), F32),
        ),
        in_specs=[
            pl.BlockSpec((2, D, 128), lambda i: (i, 0, 0)),
            pl.BlockSpec((1, D, 128), lambda i: (16 + i, 0, 0)),
            pl.BlockSpec((2, 128, 128), lambda i: (12, i, 0)),
            pl.BlockSpec((1, D, 128), lambda i: (26, 0, 0)),
            whole(UTT, 128), whole(1, D), whole(1, D),
        ],
        out_specs=[
            pl.BlockSpec((D, 256), lambda i: (0, i)),
            pl.BlockSpec((D, 128), lambda i: (0, i)),
            pl.BlockSpec((128, V), lambda i: (i, 0)),
            whole(TAPS, D), whole(1, D), whole(1, D), SM,
        ],
        scratch_shapes=[pltpu.VMEM((8, 128), F32)],
    )(total, total, total, total, loss, gain_conv.reshape(1, D), gain_out.reshape(1, D))
    win, wout, hw, depth, gain1, gain2, utt = outs
    return gain1.reshape(D), win, depth, wout, gain2.reshape(D), hw, utt


def on_device(
    features, teacher_logits, lengths, gain_conv, weight_in, weight_depth, weight_out, gain_out, head_weight
):
    got = lax.ppermute(teacher_logits, "member", ((0, 1), (1, 0)))
    grads, loss = compute(
        features, teacher_logits, got, lengths, gain_conv, weight_in, weight_depth, weight_out, gain_out,
        head_weight,
    )
    return finish(reduce_all(grads), loss, gain_conv, gain_out)


def solution(mesh):
    in_specs = (
        P(("dp", "member"), None, None), P("member", "dp", None, None), P(("dp", "member")),
        P(), P(), P(), P(), P(), P(),
    )
    out_specs = (P(), P(), P(), P(), P(), P(), P(("dp", "member")))
    return jax.shard_map(on_device, mesh=mesh, in_specs=in_specs, out_specs=out_specs, check_vma=False)
```

```python
import functools
import math

import jax
import jax.numpy as jnp
import numpy as np
from jax import lax
from jax.experimental import pallas as pl
from jax.experimental.pallas import tpu as pltpu
from jax.sharding import PartitionSpec as P

D, V, TAPS, FRAMES, UTT = 1024, 256, 31, 256, 2
TOK = UTT * FRAMES
PERIOD, HALF, ROWS = 272, 144, 288
TILE = 256
SLABS = 28
F32, BF16 = jnp.float32, jnp.bfloat16
VM = pl.BlockSpec(memory_space=pltpu.VMEM)
SM = pl.BlockSpec(memory_space=pltpu.SMEM)


def transforms():
    freq = np.arange(PERIOD // 2 + 1)
    time = np.arange(FRAMES)
    angle = 2 * np.pi * np.outer(freq, time) / PERIOD
    analysis = np.zeros((ROWS, FRAMES))
    analysis[: freq.size] = np.cos(angle)
    analysis[HALF : HALF + freq.size] = np.sin(angle)
    lag = np.arange(TAPS) - TAPS // 2
    weight = np.where((freq == 0) | (freq == PERIOD // 2), 1.0, 2.0)[:, None] / PERIOD
    turn = 2 * np.pi * np.outer(freq, lag) / PERIOD
    taps = np.zeros((ROWS, TAPS + 1))
    taps[: freq.size, :TAPS] = np.cos(turn) * weight
    taps[HALF : HALF + freq.size, :TAPS] = np.sin(turn) * weight
    lags = np.zeros((ROWS, 128))
    lags[:, : TAPS + 1] = taps
    bf = lambda v: jnp.asarray(v, F32).astype(BF16)
    return bf(analysis), bf(analysis.T), jnp.asarray(taps, F32), bf(lags)


def dot(a, b):
    return jnp.dot(a, b, preferred_element_type=F32)


def dot_bt(a, b):
    return lax.dot_general(a, b, (((1,), (1,)), ((), ())), preferred_element_type=F32)


def dot_at(a, b):
    return lax.dot_general(a, b, (((0,), (0,)), ((), ())), preferred_element_type=F32)


def sigmoid(v):
    return 1.0 / (1.0 + jnp.exp(-v))


def rows_loop(total, step, body):
    def run(i, c):
        body(pl.ds(pl.multiple_of(i * step, step), step), i)
        return c

    lax.fori_loop(0, total // step, run, 0)


def forward_kernel(
    len_ref, x_ref, g1_ref, win_ref, taps_ref, wout_ref, g2_ref, head_ref, tm_ref, c_ref, ct_ref,
    normed_ref, a_ref, s_ref, spec_ref, fac_ref, act_ref, z_ref, rstd_ref, fn_ref, logit_ref,
    taps32, res,
):
    taps32[...] = jnp.zeros_like(taps32)
    taps32[0:TAPS, :] = taps_ref[...]

    def norm_rows(rows, i):
        v = x_ref[rows, :].astype(F32)
        v = v - jnp.mean(v, axis=-1, keepdims=True)
        v = v * lax.rsqrt(jnp.mean(v * v, axis=-1, keepdims=True) + 1e-5)
        normed_ref[rows, :] = (v * g1_ref[...]).astype(BF16)

    rows_loop(TOK, 32, norm_rows)

    def channel_tile(cb, carry):
        cols = pl.ds(pl.multiple_of(cb * TILE, TILE), TILE)
        gate_cols = pl.ds(pl.multiple_of(D + cb * TILE, TILE), TILE)
        hat = jnp.dot(
            tm_ref[...], taps32[:, cols], preferred_element_type=F32, precision=lax.Precision.HIGHEST
        )
        hr, hi = hat[:HALF], hat[HALF:]
        for u in range(UTT):
            rows = pl.ds(u * FRAMES, FRAMES)
            live = lax.broadcasted_iota(jnp.int32, (FRAMES, TILE), 0) < len_ref[u]
            nu = normed_ref[rows, :]
            a = dot(nu, win_ref[:, cols])
            s = sigmoid(dot(nu, win_ref[:, gate_cols]))
            a = jnp.where(live, a, 0.0)
            s_ref[rows, cols] = s.astype(BF16)
            a_ref[rows, cols] = a.astype(BF16)
            sp = dot(c_ref[...], (a * s).astype(BF16))
            spec_ref[u, :, cols] = sp.astype(BF16)
            xr, xi = sp[:HALF], sp[HALF:]
            prod = jnp.concatenate([xr * hr + xi * hi, xi * hr - xr * hi], axis=0)
            conv = dot(ct_ref[...], prod.astype(BF16))
            sg = sigmoid(conv)
            act_ref[rows, cols] = (conv * sg).astype(BF16)
            fac_ref[rows, cols] = (sg * (1.0 + conv * (1.0 - sg))).astype(BF16)
        return carry

    lax.fori_loop(0, D // TILE, channel_tile, 0)

    def out_tile(cb, carry):
        cols = pl.ds(pl.multiple_of(cb * TILE, TILE), TILE)
        res[:, cols] = x_ref[:, cols].astype(F32) + dot(act_ref[...], wout_ref[:, cols])
        return carry

    lax.fori_loop(0, D // TILE, out_tile, 0)

    def norm_out(rows, i):
        v = res[rows, :]
        v = v - jnp.mean(v, axis=-1, keepdims=True)
        r = lax.rsqrt(jnp.mean(v * v, axis=-1, keepdims=True) + 1e-5)
        z = v * r
        z_ref[rows, :] = z.astype(BF16)
        rstd_ref[rows, :] = jnp.broadcast_to(r, (32, 128))
        fn_ref[rows, :] = (z * g2_ref[...]).astype(BF16)

    rows_loop(TOK, 32, norm_out)
    logit_ref[...] = dot(fn_ref[...], head_ref[...])


def softmax_parts(v):
    m = jnp.max(v, axis=-1, keepdims=True)
    e = jnp.exp(v - m)
    return m, e, jnp.sum(e, axis=-1, keepdims=True)


def backward_kernel(
    len_ref, own_ref, got_ref, logit_ref, fn_ref, z_ref, rstd_ref, act_ref, fac_ref, spec_ref, s_ref, a_ref,
    normed_ref, win_ref, taps_ref, wout_ref, g2_ref, head_ref, tm_ref, c_ref, ct_ref, lag_ref,
    grad_ref, loss_ref,
    taps32, dl, dz, dr, dp, gain1, left,
):
    taps32[...] = jnp.zeros_like(taps32)
    taps32[0:TAPS, :] = taps_ref[...]
    gain1[...] = jnp.zeros_like(gain1)
    first = lax.axis_index("member") * UTT

    for u in range(UTT):
        length = len_ref[u]

        def loss_rows(i, total):
            rows = pl.ds(pl.multiple_of(i * 32, 32), 32)
            flat = pl.ds(pl.multiple_of(u * FRAMES + i * 32, 32), 32)
            summed = jnp.zeros((32, V), F32)
            for ref in (own_ref, got_ref):
                for k in range(2):
                    t = ref[k, first + u, rows, :].astype(F32)
                    m, _, z = softmax_parts(t)
                    summed = summed + (t - m - jnp.log(z))
            _, e, z = softmax_parts(summed * 0.25)
            target = e / z
            lg = logit_ref[flat, :]
            m, e, z = softmax_parts(lg)
            live = i * 32 + lax.broadcasted_iota(jnp.int32, (32, V), 0) < length
            ce = jnp.sum(jnp.where(live, target * (m + jnp.log(z) - lg), 0.0), axis=0, keepdims=True)
            mass = jnp.sum(target, axis=-1, keepdims=True)
            dl[flat, :] = jnp.where(live, e * (mass / z) - target, 0.0).astype(BF16)
            return total + ce

        total = lax.fori_loop(0, FRAMES // 32, loss_rows, jnp.zeros((1, V), F32))
        loss_ref[u : u + 1, :] = jnp.broadcast_to(jnp.sum(total, axis=-1, keepdims=True), (1, 128))

    def head_tile(cb, carry):
        cols = pl.ds(pl.multiple_of(cb * TILE, TILE), TILE)
        rows = cols
        dz[:, cols] = dot_bt(dl[...], head_ref[rows, :])
        dh = dot_at(fn_ref[:, cols], dl[...])
        grad_ref[24, rows, :] = dh[:, :128].astype(BF16)
        grad_ref[25, rows, :] = dh[:, 128:].astype(BF16)
        left[1, rows, :] = jnp.broadcast_to(
            jnp.sum(dh * head_ref[rows, :].astype(F32), axis=-1, keepdims=True), (TILE, 128)
        )
        return carry

    lax.fori_loop(0, D // TILE, head_tile, 0)

    def norm_rows(rows, i):
        g = dz[rows, :] * g2_ref[...]
        z = z_ref[rows, :].astype(F32)
        r = rstd_ref[rows, :][:, :1]
        m1 = jnp.mean(g, axis=-1, keepdims=True)
        m2 = jnp.mean(g * z, axis=-1, keepdims=True)
        dr[rows, :] = (r * (g - m1 - z * m2)).astype(BF16)

    rows_loop(TOK, 32, norm_rows)

    def conv_tile(cb, carry):
        cols = pl.ds(pl.multiple_of(cb * TILE, TILE), TILE)
        gate_cols = pl.ds(pl.multiple_of(D + cb * TILE, TILE), TILE)
        hat = jnp.dot(
            tm_ref[...], taps32[:, cols], preferred_element_type=F32, precision=lax.Precision.HIGHEST
        )
        hr, hi = hat[:HALF], hat[HALF:]
        q = jnp.zeros((ROWS, TILE), F32)
        for u in range(UTT):
            rows = pl.ds(u * FRAMES, FRAMES)
            dact = dot_bt(dr[rows, :], wout_ref[cols, :])
            dc = (dact * fac_ref[rows, cols].astype(F32)).astype(BF16)
            sp = dot(c_ref[...], dc)
            er, ei = sp[:HALF], sp[HALF:]
            x = spec_ref[u, :, cols].astype(F32)
            xr, xi = x[:HALF], x[HALF:]
            q = q + jnp.concatenate([er * xr + ei * xi, er * xi - ei * xr], axis=0)
            back = jnp.concatenate([er * hr - ei * hi, ei * hr + er * hi], axis=0)
            dg = dot(ct_ref[...], back.astype(BF16))
            live = lax.broadcasted_iota(jnp.int32, (FRAMES, TILE), 0) < len_ref[u]
            s = s_ref[rows, cols].astype(F32)
            a = a_ref[rows, cols].astype(F32)
            ds = jnp.where(live, dg * s, 0.0)
            dp[rows, cols] = ds.astype(BF16)
            dp[rows, gate_cols] = (ds * a * (1.0 - s)).astype(BF16)
        left[0, cols, :] = dot_at(q.astype(BF16), lag_ref[...])
        dw = dot_at(act_ref[:, cols], dr[...])
        for j in range(8):
            grad_ref[16 + j, cols, :] = dw[:, j * 128 : (j + 1) * 128].astype(BF16)
        return carry

    lax.fori_loop(0, D // TILE, conv_tile, 0)

    def in_tile(n, carry):
        cols = pl.ds(pl.multiple_of(n * TILE, TILE), TILE)
        dw = dot_at(normed_ref[...], dp[:, cols])
        grad_ref[2 * n] = dw[:, :128].astype(BF16)
        grad_ref[2 * n + 1] = dw[:, 128:].astype(BF16)
        w = dw * win_ref[:, cols].astype(F32)
        gain1[...] += w[:, :128] + w[:, 128:]
        return carry

    lax.fori_loop(0, 2 * D // TILE, in_tile, 0)

    count = len_ref[0] + len_ref[1]

    def small_rows(rows, i):
        lane = lax.broadcasted_iota(jnp.int32, (128, 128), 1)
        bit = jnp.right_shift(count, jnp.clip(lane - 64, 0, 15)) & 1
        g1 = jnp.sum(gain1[rows, :], axis=-1, keepdims=True)
        out = jnp.where(lane < TAPS, left[0, rows, :], 0.0)
        out = jnp.where(lane == 32, g1, out)
        out = jnp.where(lane == 33, left[1, rows, :], out)
        out = jnp.where((lane >= 64) & (lane < 74), bit.astype(F32), out)
        grad_ref[26, rows, :] = out.astype(BF16)
        grad_ref[27, rows, :] = jnp.zeros((128, 128), BF16)

    rows_loop(D, 128, small_rows)


def compute(features, own, got, lengths, gain_conv, weight_in, weight_depth, weight_out, gain_out, head):
    analysis, synthesis, tapm, lagm = transforms()
    sd = jax.ShapeDtypeStruct
    cp = pltpu.CompilerParams(vmem_limit_bytes=60 << 20)
    g1, g2 = gain_conv.reshape(1, D), gain_out.reshape(1, D)
    fwd = pl.pallas_call(
        forward_kernel,
        name="forward",
        out_shape=(
            sd((TOK, D), BF16), sd((TOK, D), BF16), sd((TOK, D), BF16), sd((UTT, ROWS, D), BF16),
            sd((TOK, D), BF16), sd((TOK, D), BF16), sd((TOK, D), BF16), sd((TOK, 128), F32),
            sd((TOK, D), BF16), sd((TOK, V), F32),
        ),
        in_specs=[SM] + [VM] * 10,
        out_specs=[VM] * 10,
        scratch_shapes=[pltpu.VMEM((32, D), F32), pltpu.VMEM((TOK, D), F32)],
        compiler_params=cp,
        cost_estimate=pl.CostEstimate(flops=4 * 10**9, bytes_accessed=20 << 20, transcendentals=2 << 20),
    )
    normed, a, s, spec, fac, act, z, rstd, fn, logit = fwd(
        lengths, features.reshape(TOK, D), g1, weight_in, weight_depth, weight_out, g2, head,
        tapm, analysis, synthesis,
    )
    bwd = pl.pallas_call(
        backward_kernel,
        name="backward",
        out_shape=(sd((SLABS, D, 128), BF16), sd((UTT, 128), F32)),
        in_specs=[SM] + [VM] * 21,
        out_specs=[VM] * 2,
        scratch_shapes=[
            pltpu.VMEM((32, D), F32), pltpu.VMEM((TOK, V), BF16), pltpu.VMEM((TOK, D), F32),
            pltpu.VMEM((TOK, D), BF16), pltpu.VMEM((TOK, 2 * D), BF16), pltpu.VMEM((D, 128), F32),
            pltpu.VMEM((2, D, 128), F32),
        ],
        compiler_params=cp,
    )
    return bwd(
        lengths, own, got, logit, fn, z, rstd, act, fac, spec, s, a, normed, weight_in, weight_depth,
        weight_out, g2, head, tapm, analysis, synthesis, lagm,
    )


MESH = pl.DeviceIdType.MESH
STREAMS = 12
COUNTS = (2, 1, 1, 1, 1, 1, 1, 2, 1, 1, 1, 1)
OFFSETS = (0, 2, 3, 4, 5, 6, 7, 8, 10, 11, 12, 13)
OWN = 14
ROUNDS = 6


def position():
    member, dp = lax.axis_index("member"), lax.axis_index("dp")
    core, z, rest = dp % 2, (dp // 2) % 4, dp // 8
    return ((rest % 2) * 2 + member, rest // 2, z), core


def device(coords, core):
    x, y, z = coords
    return {"member": x % 2, "dp": ((y * 2 + x // 2) * 4 + z) * 2 + core}


def other(c, wide):
    return 3 - c if wide else c + 1 - 2 * (c % 2)


def kept(c, kind, second):
    if kind == 0 and not second:
        return (c + c // 2) % 2
    return c % 2 if (kind == 1 and second) else c // 2


def route(coords, core, s, k):
    s = s % 6
    dim = (s // 2 + core + k // 2) % 3
    hit = [jnp.where(dim == d, 1, 0) for d in range(3)]
    c = sum(h * v for h, v in zip(hit, coords))
    kind, second = s % 2, k % 2
    p = other(c, (kind + second) % 2 == 1)
    peer = [v + h * (p - v) for h, v in zip(hit, coords)]
    return device(peer, core), kept(c, kind, second == 1)


def reduce_kernel(
    grad_ref, out_ref, pair_buf, work, *rest
):
    bufs = rest[:ROUNDS]
    pair_s, pair_r, rs_s, rs_r, ag_s, ag_r, fin_s, fin_r = rest[ROUNDS:]
    coords, core = position()
    partner = device(coords, 1 - core)
    mine = core * OWN
    theirs = (1 - core) * OWN

    barrier = pltpu.get_barrier_semaphore()
    greet = [partner]
    for d in range(3):
        for wide in (False, True):
            greet.append(device([other(v, wide) if i == d else v for i, v in enumerate(coords)], core))
    for dev in greet:
        pl.semaphore_signal(barrier, inc=1, device_id=dev, device_id_type=MESH)
    pl.semaphore_wait(barrier, len(greet))

    def copy(src, dst, send, recv, dev):
        return pltpu.make_async_remote_copy(
            src_ref=src, dst_ref=dst, send_sem=send, recv_sem=recv, device_id=dev, device_id_type=MESH
        )

    pending = []
    pairs = []
    for s in range(STREAMS):
        off, n = OFFSETS[s], COUNTS[s]
        c = copy(
            grad_ref.at[pl.ds(theirs + off, n)], pair_buf.at[pl.ds(off, n)], pair_s.at[s], pair_r.at[s], partner
        )
        c.start()
        pairs.append(c)

    starts = [jnp.int32(0)] * STREAMS
    history = [[] for _ in range(STREAMS)]
    flying = [None] * STREAMS

    def launch(s, k):
        half = 512 >> k
        dev, keep = route(coords, core, s, k)
        slots = pl.ds(OFFSETS[s], COUNTS[s])
        give = pl.multiple_of(starts[s] + (1 - keep) * half, 16)
        c = copy(
            work.at[slots, pl.ds(give, half)],
            bufs[k].at[pl.ds(OFFSETS[s], COUNTS[s])],
            rs_s.at[s, k], rs_r.at[s, k], dev,
        )
        c.start()
        flying[s] = c
        pending.append(c)
        starts[s] = starts[s] + keep * half
        history[s].append(dev)

    def add(dst_ref, dst_slot, dst_row, a_ref, a_slot, a_row, b_ref, b_slot, n, size):
        step = min(size, 128)

        def run(i, carry):
            r = i * step
            for j in range(n):
                d = pl.ds(pl.multiple_of(dst_row + r, 16), step)
                a = a_ref[a_slot + j, pl.ds(pl.multiple_of(a_row + r, 16), step), :]
                b = b_ref[b_slot + j, pl.ds(pl.multiple_of(r, 16), step), :]
                dst_ref[dst_slot + j, d, :] = a + b
            return carry

        lax.fori_loop(0, size // step, run, 0)

    for s in range(STREAMS):
        off, n = OFFSETS[s], COUNTS[s]
        pairs[s].wait_recv()
        add(work, off, 0, grad_ref, mine + off, 0, pair_buf, off, n, D)
        launch(s, 0)

    for k in range(ROUNDS):
        half = 512 >> k
        for s in range(STREAMS):
            off, n = OFFSETS[s], COUNTS[s]
            flying[s].wait_recv()
            if k + 1 < ROUNDS:
                add(work, off, starts[s], work, off, starts[s], bufs[k], off, n, half)
                launch(s, k + 1)
            else:
                add(out_ref, mine + off, starts[s], work, off, starts[s], bufs[k], off, n, half)
                gather(s, k, copy, out_ref, mine, starts, history, ag_s, ag_r, flying, pending)

    handed = []

    def hand(s, part, start):
        span = pl.ds(pl.multiple_of(start, 16), 512)
        slots = pl.ds(mine + OFFSETS[s], COUNTS[s])
        c = copy(
            out_ref.at[slots, span], out_ref.at[slots, span], fin_s.at[part, s], fin_r.at[part, s], partner
        )
        c.start()
        handed.append(c)

    for k in range(ROUNDS - 1, -1, -1):
        half = 512 >> k
        for s in range(STREAMS):
            flying[s].wait_recv()
            _, keep = route(coords, core, s, k)
            before = starts[s]
            starts[s] = before - keep * half
            if k > 0:
                gather(s, k - 1, copy, out_ref, mine, starts, history, ag_s, ag_r, flying, pending)
                if k == 1:
                    hand(s, 0, starts[s])
            else:
                hand(s, 1, 512 - before)
    for c in handed:
        c.wait_recv()
        c.wait_send()
    for s in range(STREAMS):
        pairs[s].wait_send()
    for c in pending:
        c.wait_send()


def gather(s, k, copy, out_ref, mine, starts, history, ag_s, ag_r, flying, pending):
    half = 512 >> k
    slots = pl.ds(mine + OFFSETS[s], COUNTS[s])
    span = pl.ds(pl.multiple_of(starts[s], 16), half)
    c = copy(
        out_ref.at[slots, span], out_ref.at[slots, span], ag_s.at[s, k], ag_r.at[s, k], history[s][k]
    )
    c.start()
    flying[s] = c
    pending.append(c)


def reduce_all(grads):
    dma = pltpu.SemaphoreType.DMA
    return pl.pallas_call(
        reduce_kernel,
        name="reduce_all",
        out_shape=jax.ShapeDtypeStruct((SLABS, D, 128), BF16),
        in_specs=[VM],
        out_specs=VM,
        scratch_shapes=[pltpu.VMEM((OWN, D, 128), BF16)] * 2
        + [pltpu.VMEM((OWN, 512 >> k, 128), BF16) for k in range(ROUNDS)]
        + [dma((STREAMS,))] * 2 + [dma((STREAMS, ROUNDS))] * 4 + [dma((2, STREAMS))] * 2,
        compiler_params=pltpu.CompilerParams(
            collective_id=0, has_side_effects=True, vmem_limit_bytes=48 << 20
        ),
    )(grads)


def finish_kernel(
    in_ref, mid_ref, head_ref, small_ref, loss_ref, g1_ref, g2_ref,
    win_ref, wout_ref, hw_ref, depth_ref, gain1_ref, gain2_ref, utt_ref, scale,
):
    @pl.when(pl.program_id(0) == 0)
    def _():
        first = small_ref[0, 0:16, :].astype(F32)[0:1, :]
        lane = lax.broadcasted_iota(jnp.int32, (1, 128), 1)
        place = jnp.left_shift(1, jnp.clip(lane - 64, 0, 12)).astype(F32)
        used = (lane >= 64) & (lane < 74)
        count = jnp.sum(jnp.where(used, first * place, 0.0), axis=-1, keepdims=True)
        inv = UTTS / count
        scale[...] = jnp.broadcast_to(inv, (8, 128))
        for u in range(UTT):
            utt_ref[u] = jnp.max(loss_ref[u : u + 1, :] * inv)
        small = small_ref[0].astype(F32).T * inv
        depth_ref[...] = small[0:TAPS, :]
        gain1_ref[...] = small[32:33, :] / g1_ref[...]
        gain2_ref[...] = small[33:34, :] / g2_ref[...]

    inv = scale[0:1, :]
    for src, dst, n in ((in_ref, win_ref, 16), (mid_ref, wout_ref, 8), (head_ref, hw_ref, 2)):
        for j in range(n):
            dst[:, j * 128 : (j + 1) * 128] = src[j].astype(F32) * inv


UTTS = 256.0


def finish(total, loss, gain_conv, gain_out):
    sd = jax.ShapeDtypeStruct
    whole = lambda *shape: pl.BlockSpec(shape, lambda i: (0,) * len(shape))
    outs = pl.pallas_call(
        finish_kernel,
        name="finish",
        grid=(8,),
        out_shape=(
            sd((D, 2 * D), F32), sd((D, D), F32), sd((D, V), F32), sd((TAPS, D), F32),
            sd((1, D), F32), sd((1, D), F32), sd((UTT,), F32),
        ),
        in_specs=[
            pl.BlockSpec((16, 128, 128), lambda i: (0, i, 0)),
            pl.BlockSpec((8, 128, 128), lambda i: (2, i, 0)),
            pl.BlockSpec((2, 128, 128), lambda i: (12, i, 0)),
            pl.BlockSpec((1, D, 128), lambda i: (26, 0, 0)),
            whole(UTT, 128), whole(1, D), whole(1, D),
        ],
        out_specs=[
            pl.BlockSpec((128, 2 * D), lambda i: (i, 0)),
            pl.BlockSpec((128, D), lambda i: (i, 0)),
            pl.BlockSpec((128, V), lambda i: (i, 0)),
            whole(TAPS, D), whole(1, D), whole(1, D), SM,
        ],
        scratch_shapes=[pltpu.VMEM((8, 128), F32)],
    )(total, total, total, total, loss, gain_conv.reshape(1, D), gain_out.reshape(1, D))
    win, wout, hw, depth, gain1, gain2, utt = outs
    return gain1.reshape(D), win, depth, wout, gain2.reshape(D), hw, utt


def on_device(
    features, teacher_logits, lengths, gain_conv, weight_in, weight_depth, weight_out, gain_out, head_weight
):
    got = lax.ppermute(teacher_logits, "member", ((0, 1), (1, 0)))
    grads, loss = compute(
        features, teacher_logits, got, lengths, gain_conv, weight_in, weight_depth, weight_out, gain_out,
        head_weight,
    )
    return finish(reduce_all(grads), loss, gain_conv, gain_out)


def solution(mesh):
    in_specs = (
        P(("dp", "member"), None, None), P("member", "dp", None, None), P(("dp", "member")),
        P(), P(), P(), P(), P(), P(),
    )
    out_specs = (P(), P(), P(), P(), P(), P(), P(("dp", "member")))
    return jax.shard_map(on_device, mesh=mesh, in_specs=in_specs, out_specs=out_specs, check_vma=False)
```
